512 devices in a mesh: slab: 16 (over z, core), dom: 32 (over x, y).
Axes of the slice: x: 4, y: 8, z: 8, core: 2. Of those that a mesh axis runs over, the one named last changes fastest.
Arguments:
- positions: float32 [3, 262144], P(None, ('slab', 'dom')), may hold values from -0.5 to 64.5, as said below
- burgers: float32 [3, 262144], P(None, ('slab', 'dom')), may hold values from -6 to 6
- mobility: float32 [262144], P(('slab', 'dom')), may hold values from 0.5 to 2
- block_cells: int32 [2048], P(('slab', 'dom')), may hold values from 0 to 255, as said below
- pairs: int32 [32768, 2], P(('slab', 'dom')), may hold values from 0 to 2047, as said below
- pair_count: int32 [512], P(('slab', 'dom')), may hold values from 8 to 64, as said below
Outputs:
- moved: float32 [3, 262144], P(None, ('slab', 'dom'))
- velocity: float32 [3, 262144], P(None, ('slab', 'dom'))
The draws below stay inside these ranges and needn't reach their ends.
Inputs may be any that keep to these rules, and one draw needn't show every extreme that they name: `block_cells`: block k lies in slab k // (4 * 32) and its cell is 16 times that slab plus 0 to 15. `positions`: each segment lies within 2.5 of its block's cell centre along x and within 1.5 along y and z. `pairs`: device d = s * 32 + e owns blocks d * 4 to (d + 1) * 4 - 1. In device d's slots the first block is one of its own; the second is owned by a device of slab s - 1, s or s + 1 at dom position e - 1, e or e + 1, and differs from the first. Every slot holds such a pair, used or not. `pair_count`: in each slab exactly one device has 64 used slots; the others have at most 32.
All inputs are finite; a program needn't handle non-finite values.
Results may differ from the reference program's by a relative error of at most 0.0003.
Values sent between devices are 32-bit elements; how exact they have to be, the bound alone decides.
A program may use at most 64 MiB of HBM per device.

```python
import math
import jax
import jax.numpy as jnp
from jax import lax

BLOCK_SEGS = 128
BLK_DEV = 4
MOST_BLOCK_PAIRS = 64
BLOCKS = 2048
SEGS = 262144
CELLS = 256
N_SLAB = 16
N_DOM = 32


def cell_helper(key):
    count = BLK_DEV * N_SLAB * N_DOM
    sub = jax.random.fold_in(key, 11)
    slabs = jnp.arange(count, dtype=jnp.int32) // (BLK_DEV * N_DOM)
    return (slabs * 16 + jax.random.randint(sub, (count,), 0, 16)).astype(jnp.int32)


def draw_block_cells(key, part):
    return cell_helper(key)


def draw_positions(key, part):
    cells = cell_helper(key)
    count = cells.shape[0]
    slabs = cells // 16
    rest = cells % 16
    centre = jnp.stack([4 * slabs + 2, 2 * (rest // 4) + 1, 2 * (rest % 4) + 1]).astype(jnp.float32)
    first, second = jax.random.split(jax.random.fold_in(key, 12))
    spread = jnp.array([2.0, 1.0, 1.0], jnp.float32)[:, None]
    block_mid = centre + jax.random.uniform(first, (3, count), jnp.float32, -1.0, 1.0) * spread
    inner = jax.random.uniform(second, (3, count, BLOCK_SEGS), jnp.float32, -0.5, 0.5)
    return (block_mid[:, :, None] + inner).reshape(3, count * BLOCK_SEGS)


def draw_pairs(key, part):
    total = N_SLAB * N_DOM * MOST_BLOCK_PAIRS
    rows = jnp.arange(total, dtype=jnp.int32)
    owner = rows // MOST_BLOCK_PAIRS
    slabs = owner // N_DOM
    doms = owner % N_DOM
    kfirst, kslab, kdom, kblock = jax.random.split(jax.random.fold_in(key, 31), 4)
    first = owner * BLK_DEV + jax.random.randint(kfirst, (total,), 0, BLK_DEV)
    other_slab = jnp.clip(slabs + jax.random.randint(kslab, (total,), -1, 2), 0, N_SLAB - 1)
    other_dom = jnp.clip(doms + jax.random.randint(kdom, (total,), -1, 2), 0, N_DOM - 1)
    second = (other_slab * N_DOM + other_dom) * BLK_DEV + jax.random.randint(kblock, (total,), 0, BLK_DEV)
    spare_dom = jnp.where(doms < N_DOM - 1, doms + 1, doms - 1)
    spare = (slabs * N_DOM + spare_dom) * BLK_DEV + first % BLK_DEV
    second = jnp.where(second == first, spare, second)
    return jnp.stack([first, second], axis=1).astype(jnp.int32)


def draw_pair_count(key, part):
    device_list = N_SLAB * N_DOM
    heated_key, lowest_key = jax.random.split(jax.random.fold_in(key, 21))
    hot = jax.random.randint(heated_key, (N_SLAB,), 0, N_DOM)
    index = jnp.arange(device_list, dtype=jnp.int32)
    slabs = index // N_DOM
    doms = index % N_DOM
    lower_bound = jax.random.randint(lowest_key, (device_list,), MOST_BLOCK_PAIRS // 8, MOST_BLOCK_PAIRS // 2 + 1)
    return jnp.where(doms == hot[slabs], MOST_BLOCK_PAIRS, lower_bound).astype(jnp.int32)


def steps_of(stream_key, extent, shards, least, top_value):
    factor_of = 1.0
    for position, parts in shards:
        heights = jax.random.uniform(jax.random.fold_in(jax.random.fold_in(stream_key, 6), position), (parts,), jnp.float32, least / len(shards), top_value / len(shards))
        factor_of = factor_of * jnp.repeat(jnp.exp(heights), extent[position] // parts).reshape((-1,) + (1,) * (len(extent) - 1 - position))
    return factor_of


def bell_draw(rng, dims, scale, bound, cuts=(), kind=jnp.bfloat16):
    result = scale * jax.random.normal(rng, dims, jnp.float32)
    if cuts:
        result = result * steps_of(rng, dims, cuts, -0.22, 0.18)
    return jnp.clip(result, -bound, bound).astype(kind)


def setup_inputs(seed: int = 0) -> dict:
    seeds = jax.random.split(jax.random.key(seed), 7)
    positions = draw_positions(jax.random.fold_in(seeds[6], 71), 0)
    burgers = bell_draw(seeds[1], (3, SEGS), 1.0, 6.0, ((1, 512),), jnp.float32)
    mobility = jnp.clip(jnp.exp(math.log(2.0) - 1.3862944 * jax.random.uniform(seeds[2], (SEGS,), jnp.float32) ** steps_of(seeds[2], (SEGS,), ((0, 512),), -0.2, 0.2)), 0.5, 2.0)
    block_cells = draw_block_cells(jax.random.fold_in(seeds[6], 71), 0)
    pairs = draw_pairs(jax.random.fold_in(seeds[6], 71), 0)
    pair_count = draw_pair_count(jax.random.fold_in(seeds[6], 71), 0)
    return {"positions": positions, "burgers": burgers, "mobility": mobility, "block_cells": block_cells, "pairs": pairs, "pair_count": pair_count}


core_near = 0.25
core_far = 9.0
time_increment = 0.25
hi_prec = lax.Precision.HIGHEST

def centers(cells):
    whole = cells.astype(jnp.int32)
    slabs = whole // 16
    rest = whole % 16
    return jnp.stack([4 * slabs + 2, 2 * (rest // 4) + 1, 2 * (rest % 4) + 1]).astype(jnp.float32)

def block_moments(posit, burg, cells, ncells, width):
    nblk = cells.shape[0]
    offset = posit.reshape(3, nblk, width) - centers(cells)[:, :, None]
    vec = burg.reshape(3, nblk, width)
    first = (vec[:, None] * offset[None]).reshape(9, nblk, width)
    second = (vec[:, None, None] * offset[None, :, None] * offset[None, None, :]).reshape(27, nblk, width)
    rows = lax.optimization_barrier(jnp.sum(jnp.concatenate([vec, first, second], axis=0), axis=2))
    onehot = (cells[:, None] == jnp.arange(ncells, dtype=jnp.int32)[None, :]).astype(jnp.float32)
    return jnp.dot(rows, onehot, precision=hi_prec)

def far_field(posit, burg, moments):
    ncells = moments.shape[1]
    nblk = ncells // 64
    zeds = centers(jnp.arange(ncells, dtype=jnp.int32)).reshape(3, nblk, 64).transpose(1, 0, 2)
    mblk = moments.reshape(39, nblk, 64).transpose(1, 0, 2)

    def visit(acc, item):
        zpart, mpart = item
        r = posit[:, None, :] - zpart[:, :, None]
        sq = r[0] * r[0] + r[1] * r[1] + r[2] * r[2] + core_far
        inv3 = 1.0 / (sq * jnp.sqrt(sq))
        inv5 = inv3 / sq
        inv7 = inv5 / sq
        qzero = jnp.einsum('kc,kn->cn', mpart[0:3], burg, precision=hi_prec)
        qone = jnp.einsum('kac,kn->acn', mpart[3:12].reshape(3, 3, 64), burg, precision=hi_prec)
        qtwo = jnp.einsum('kabc,kn->abcn', mpart[12:39].reshape(3, 3, 3, 64), burg, precision=hi_prec)
        qone_r = lax.optimization_barrier(jnp.sum(qone * r, axis=0))
        qtwo_r = lax.optimization_barrier(jnp.sum(qtwo * r[None], axis=1))
        rqr = lax.optimization_barrier(jnp.sum(r * qtwo_r, axis=0))
        trace = qtwo[0, 0] + qtwo[1, 1] + qtwo[2, 2]
        scal = qzero * inv3 + 3.0 * qone_r * inv5 - 1.5 * trace * inv5 + 7.5 * rqr * inv7
        force = r * scal[None] - qone * inv3[None] - 3.0 * qtwo_r * inv5[None]
        return (acc + lax.optimization_barrier(jnp.sum(force, axis=1)), None)
    start = jnp.zeros(posit.shape, jnp.float32)
    total, unused = lax.scan(visit, start, (zeds, mblk))
    return total

def pair_forces(pos_a, bur_a, pos_b, bur_b, weight):
    r = pos_a[:, :, :, None] - pos_b[:, :, None, :]
    sq = r[0] * r[0] + r[1] * r[1] + r[2] * r[2]
    near_s = sq + core_near
    far_s = sq + core_far
    kern = 1.0 / (near_s * jnp.sqrt(near_s)) - 1.0 / (far_s * jnp.sqrt(far_s))
    coef = lax.optimization_barrier(jnp.sum(bur_a[:, :, :, None] * bur_b[:, :, None, :], axis=0))
    wgt = weight[:, None, None] * coef * kern
    wr = wgt[None] * r
    return (lax.optimization_barrier(jnp.sum(wr, axis=3)), -lax.optimization_barrier(jnp.sum(wr, axis=2)))

def reference(positions, burgers, mobility, block_cells, pairs, pair_count):
    device_list = N_SLAB * N_DOM
    width = BLOCK_SEGS
    per_dev = BLK_DEV * BLOCK_SEGS
    far_scale = math.sqrt(CELLS / SEGS)

    def speed(posit):
        moments = block_moments(posit, burgers, block_cells, CELLS, width)
        pdev = posit.reshape(3, device_list, per_dev).transpose(1, 0, 2)
        bdev = burgers.reshape(3, device_list, per_dev).transpose(1, 0, 2)
        far = lax.map(lambda item: far_field(item[0], item[1], moments), (pdev, bdev))
        far = far.transpose(1, 0, 2).reshape(3, -1)
        pblk = posit.reshape(3, BLOCKS, width)
        bblk = burgers.reshape(3, BLOCKS, width)

        def visit(acc, item):
            plist, count = item
            weight = (jnp.arange(MOST_BLOCK_PAIRS, dtype=jnp.int32) < count).astype(jnp.float32)
            first = plist[:, 0]
            second = plist[:, 1]
            force_a, force_b = pair_forces(pblk[:, first], bblk[:, first], pblk[:, second], bblk[:, second], weight)
            return (acc.at[:, first].add(force_a).at[:, second].add(force_b), None)
        start = jnp.zeros((3, BLOCKS, width), jnp.float32)
        near, unused = lax.scan(visit, start, (pairs.reshape(device_list, MOST_BLOCK_PAIRS, 2), pair_count))
        return mobility[None, :] * (far_scale * far + near.reshape(3, -1))
    first_v = speed(positions)
    second_v = speed(positions + time_increment * first_v)
    total = first_v + second_v
    return (positions + 0.5 * time_increment * total, 0.5 * total)
```

```python
import functools
import math

import jax
import jax.numpy as jnp
from jax import lax
from jax.experimental import pallas as pl
from jax.experimental.pallas import tpu as pltpu
from jax.sharding import PartitionSpec as P

MESH = pl.DeviceIdType.MESH
F32 = jnp.float32
BF16 = jnp.bfloat16

BLK = 4
LANES = 128
SLOTS = 64
OWN = 16
UNROLL = 4
core_far = 9.0
time_increment = 0.25
around = [(ds, de) for ds in (-1, 0, 1) for de in (-1, 0, 1) if (ds, de) != (0, 0)]


def split3(x):
    hi = x.astype(BF16).astype(F32)
    rest = x - hi
    mid = rest.astype(BF16).astype(F32)
    return hi, mid, rest - mid


def left_stack(parts):
    hi, mid, lo = parts
    return jnp.concatenate([hi, hi, mid, hi, mid, lo], axis=0)


def right_stack(parts):
    hi, mid, lo = parts
    return jnp.concatenate([hi, mid, hi, lo, mid, hi], axis=0)


def mm(a, b, ca=1, cb=0):
    return lax.dot_general(a, b, (((ca,), (cb,)), ((), ())), preferred_element_type=F32)


def iotas():
    row = lax.broadcasted_iota(jnp.int32, (8, LANES), 0)
    lane = lax.broadcasted_iota(jnp.int32, (8, LANES), 1)
    return row, lane


def step_kernel(
    n_slab,
    n_dom,
    far_scale,
    pos_ref,
    bur_ref,
    mob_ref,
    cells_ref,
    pairs_ref,
    count_ref,
    out_ref,
    idx_a,
    idx_b,
    onehot,
    onehot_t,
    own,
    window,
    left_feat,
    right_feat,
    sums_feat,
    pair_sums,
    give,
    given,
    mom_dom,
    mom_slab,
    feats,
    feats_split,
    bur_split,
    q_buf,
    far_buf,
    pos_rows,
    mob_rows,
    send_sem,
    recv_sem,
):
    s = lax.axis_index("slab")
    e = lax.axis_index("dom")
    halves = n_slab // 8
    row, lane = iotas()
    centre_x = (4 * s + 2).astype(F32)
    centre = jnp.where(row == 0, centre_x, jnp.where(row < 3, 4.0, 0.0))

    def peer(ds, de):
        return (lax.rem(s + ds + n_slab, n_slab), lax.rem(e + de + n_dom, n_dom))

    barrier = pltpu.get_barrier_semaphore()

    def greet(slab, dom):
        pl.semaphore_signal(barrier, inc=1, device_id=(slab, dom), device_id_type=MESH)

    def greet_dom(i, c):
        greet(s, lax.rem(e + i, n_dom))
        return c

    def greet_slab(i, c):
        greet(lax.rem(s + i, n_slab), e)
        return c

    lax.fori_loop(1, n_dom, greet_dom, 0)
    lax.fori_loop(1, n_slab, greet_slab, 0)
    for ds, de in around:
        if ds != 0 and de != 0:
            greet(*peer(ds, de))

    device = s * n_dom + e
    used = count_ref[0]

    def place(t, c):
        first = pairs_ref[2 * t]
        second = pairs_ref[2 * t + 1]
        owner = second // BLK
        row_off = owner // n_dom - s + 1
        col_off = owner % n_dom - e + 1
        ia = jnp.clip(first - device * BLK, 0, BLK - 1)
        ib = jnp.clip((row_off * 3 + col_off) * BLK + second % BLK, 0, 9 * BLK - 1)
        idx_a[t] = ia
        idx_b[t] = ib
        live = t < used
        to_a = jnp.where(live, OWN + ia, LANES - 1)
        to_b = jnp.where(live, ib, LANES - 1)
        one_lane = lax.broadcasted_iota(jnp.int32, (1, LANES), 1)
        onehot[pl.ds(t, 1), :] = jnp.where(one_lane == to_a, 1.0, 0.0)
        onehot[pl.ds(SLOTS + t, 1), :] = jnp.where(one_lane == to_b, 1.0, 0.0)
        return c

    lax.fori_loop(0, SLOTS, place, 0)
    onehot_t[...] = jnp.transpose(onehot[...])[:48].astype(BF16)

    bur_tiles = []
    for b in range(BLK):
        cols = slice(b * LANES, (b + 1) * LANES)
        bur = bur_ref[:, cols]
        bur_tiles.append(bur)
        for c in range(3):
            pos_rows[c, b : b + 1, :] = pos_ref[c : c + 1, cols]
        mob_rows[b : b + 1, :] = mob_ref[:, cols]
        padded = jnp.concatenate([bur, jnp.zeros((5, LANES), F32)], axis=0)
        bur_split[:, cols] = right_stack(split3(padded)).astype(BF16)
    feats[...] = jnp.zeros(feats.shape, F32)

    def local_moments(phase):
        sums = [jnp.zeros((8, LANES), F32) for _ in range(4)]
        for b in range(BLK):
            tile = own[phase, b]
            inside = cells_ref[b] - 16 * s
            zy = (2 * (inside // 4) + 1).astype(F32)
            zz = (2 * (inside % 4) + 1).astype(F32)
            d0 = tile[0:1] - centre_x
            d1 = tile[1:2] - zy
            d2 = tile[2:3] - zz
            one = jnp.ones((1, LANES), F32)
            mono = jnp.concatenate([one, d0, d1, d2, d0 * d0, d1 * d1, d2 * d2, d0 * d1], axis=0)
            more = jnp.concatenate([d0 * d2, d1 * d2, jnp.zeros((6, LANES), F32)], axis=0)
            spot = lane == 16 * row + inside
            for k in range(3):
                bk = tile[3 + k : 4 + k]
                m = jnp.sum(mono * bk, axis=1, keepdims=True)
                sums[k] = sums[k] + jnp.where(spot, m, 0.0)
                m = jnp.sum(more * bk, axis=1, keepdims=True)
                sums[3] = sums[3] + jnp.where(lane == 16 * (row + 2 * k) + inside, m, 0.0)
        rows = [jnp.sum(x, axis=0, keepdims=True) for x in sums]
        mom_dom[phase, e] = jnp.concatenate(rows, axis=0)

    def remote(src, dst, phase, kind, target):
        return pltpu.make_async_remote_copy(
            src_ref=src,
            dst_ref=dst,
            send_sem=send_sem.at[phase, kind],
            recv_sem=recv_sem.at[phase, kind],
            device_id=target,
            device_id_type=MESH,
        )

    def start_halo(phase):
        for ds, de in around:
            slot = (1 - ds) * 3 + (1 - de)
            dst = window.at[phase, pl.ds(slot * BLK, BLK)]
            remote(own.at[phase], dst, phase, 0, peer(ds, de)).start()

    def start_dom(phase):
        def go(i, c):
            mine = mom_dom.at[phase, e]
            remote(mine, mine, phase, 1, (s, lax.rem(e + i, n_dom))).start()
            return c

        lax.fori_loop(1, n_dom, go, 0)

    def start_slab(phase):
        def go(i, c):
            mine = mom_slab.at[phase, s]
            remote(mine, mine, phase, 2, (lax.rem(s + i, n_slab), e)).start()
            return c

        lax.fori_loop(1, n_slab, go, 0)

    def start_give(phase):
        for ds, de in around:
            d = (ds + 1) * 3 + de + 1
            remote(give.at[phase, d], given.at[phase, 8 - d], phase, 3, peer(ds, de)).start()

    def extent(phase, kind):
        return (
            window.at[phase, pl.ds(0, 8 * BLK)],
            mom_dom.at[phase, pl.ds(0, n_dom - 1)],
            mom_slab.at[phase, pl.ds(0, n_slab - 1)],
            given.at[phase, pl.ds(0, 8)],
        )[kind]

    def all_of(phase, kind):
        whole = extent(phase, kind)
        return remote(whole, whole, phase, kind, peer(0, 1))

    def prepare(phase):
        def one(w, c):
            x = window[phase, w] - centre
            n = jnp.sum(jnp.where(row < 3, x * x, 0.0), axis=0, keepdims=True)
            mixed = jnp.where(row < 6, x, jnp.where(row == 6, n, 1.0))
            hi, mid, lo = split3(mixed)
            other = jnp.where(
                row < 3, -2.0 * x, jnp.where(row == 7, n + 0.25, jnp.where(row == 6, 1.0, 0.0))
            )
            right_feat[w, :, 0:LANES] = right_stack(split3(other)).astype(BF16)
            is_b = (row >= 3) & (row < 6)
            bs = [jnp.where(is_b, part, 0.0) for part in (hi, mid, lo)]
            right_feat[w, :, LANES : 2 * LANES] = right_stack(bs).astype(BF16)
            sums_feat[w] = jnp.concatenate([hi, mid], axis=0).astype(BF16)
            return c

        lax.fori_loop(0, 9 * BLK, one, 0, unroll=2)
        for b in range(BLK):
            x = own[phase, b] - centre
            n = jnp.sum(jnp.where(row < 3, x * x, 0.0), axis=0, keepdims=True)
            mixed = jnp.where(row < 6, x, jnp.where(row == 6, n, 1.0))
            left_feat[b] = jnp.transpose(left_stack(split3(mixed))).astype(BF16)

    def near(begin, end):
        def pair(t):
            ia = idx_a[t]
            ib = idx_b[t]
            both = mm(left_feat[ia], right_feat[ib])
            close = both[:, 0:LANES]
            coef = both[:, LANES : 2 * LANES]
            r1 = lax.rsqrt(close)
            r2 = lax.rsqrt(close + (core_far - 0.25))
            w = coef * (r1 * r1 * r1 - r2 * r2 * r2)
            hi = w.astype(BF16)
            lo = (w - hi.astype(F32)).astype(BF16)
            fa = sums_feat[OWN + ia]
            fb = sums_feat[ib]
            on_b = mm(fa, hi) + mm(fa, lo)
            on_a = mm(fb, hi, 1, 1) + mm(fb, lo, 1, 1)
            on_a = on_a[0:8] + on_a[8:16]
            on_b = on_b[0:8] + on_b[8:16]
            for i, r in enumerate((0, 1, 2, 7)):
                pair_sums[i, pl.ds(t, 1), :] = on_a[r : r + 1]
                pair_sums[i, pl.ds(SLOTS + t, 1), :] = on_b[r : r + 1]

        def turn(i, c):
            for u in range(UNROLL):
                pair(i * UNROLL + u)
            return c

        lax.fori_loop(begin // UNROLL, end // UNROLL, turn, 0)

    def collect(phase):
        chosen = onehot_t[...]
        acc = []
        for i in range(4):
            hi, mid, lo = split3(pair_sums[i])
            acc.append(mm(chosen, hi.astype(BF16)) + mm(chosen, mid.astype(BF16)) + mm(chosen, lo.astype(BF16)))
        blocks = lax.broadcasted_iota(jnp.int32, (48, LANES), 0)
        shift = (4 * (1 - blocks // 12)).astype(F32)
        acc[0] = acc[0] + shift * acc[3]
        for d in range(9):
            for i in range(4):
                give[phase, d, i] = acc[i][d * BLK : (d + 1) * BLK]

    def swap_groups(x):
        for d in (1, 2, 4):
            up = pltpu.roll(pltpu.roll(x, 8 - d, 0), 16 * d, 1)
            down = pltpu.roll(pltpu.roll(x, d, 0), LANES - 16 * d, 1)
            rbit = (row // d) % 2
            gbit = (lane // (16 * d)) % 2
            x = jnp.where(rbit == gbit, x, jnp.where(rbit == 0, up, down))
        return x

    def far(phase, half):
        for q in range(4):
            rows = jnp.concatenate(
                [mom_slab[phase, half * 8 + j, q : q + 1, :] for j in range(8)], axis=0
            )
            x = swap_groups(rows)
            if q < 3:
                for f in range(8):
                    feats[f, q : q + 1, :] = x[f : f + 1] * (1.0 if f < 4 else 3.0)
                feats[10, q : q + 1, :] = -1.5 * (x[4:5] + x[5:6] + x[6:7])
            else:
                for k in range(3):
                    for f in (8, 9):
                        j = 2 * k + f - 8
                        feats[f, k : k + 1, :] = x[j : j + 1] * 3.0
        for f in range(11):
            stacked = left_stack(split3(feats[f])).astype(BF16)
            q_buf[f] = mm(stacked, bur_split[...], 0, 0)

        zz = (2 * (row % 4) + 1).astype(F32)

        def group(g, acc):
            acc = list(acc)
            zx = (4 * (half * 8 + g // 2) + 2).astype(F32)
            zy = (2 * (2 * (g % 2) + row // 4) + 1).astype(F32)
            for t in range(BLK):
                cols = slice(t * LANES, (t + 1) * LANES)
                q = [q_buf[f, pl.ds(pl.multiple_of(8 * g, 8), 8), cols] for f in range(11)]
                dx = jnp.broadcast_to(far_buf[0, t : t + 1, :] - zx, (8, LANES))
                dy = far_buf[1, t : t + 1, :] - zy
                dz = far_buf[2, t : t + 1, :] - zz
                rs = lax.rsqrt(dx * dx + (dy * dy + dz * dz + core_far))
                i2 = rs * rs
                i3 = rs * i2
                qr = q[1] * dx + q[2] * dy + q[3] * dz
                tx = q[4] * dx + q[7] * dy + q[8] * dz
                ty = q[7] * dx + q[5] * dy + q[9] * dz
                tz = q[8] * dx + q[9] * dy + q[6] * dz
                rqr = tx * dx + ty * dy + tz * dz
                scal = q[0] + i2 * (3.0 * qr + q[10] + 2.5 * i2 * rqr)
                acc[t] = acc[t] + i3 * (dx * scal - q[1] - i2 * tx)
                acc[4 + t] = acc[4 + t] + i3 * (dy * scal - q[2] - i2 * ty)
                acc[8 + t] = acc[8 + t] + i3 * (dz * scal - q[3] - i2 * tz)
            return tuple(acc)

        zero = jnp.zeros((8, LANES), F32)
        return lax.fori_loop(0, 16, group, (zero,) * 12)

    def speed(phase):
        p = [far_buf[c] for c in range(3)]
        prepare(phase)
        near(0, SLOTS // 2)
        all_of(phase, 1).wait_recv()
        mom_slab[phase, s] = jnp.sum(mom_dom[phase], axis=0)
        start_slab(phase)
        near(SLOTS // 2, SLOTS)
        collect(phase)
        start_give(phase)
        all_of(phase, 2).wait_recv()
        total = None
        for half in range(halves):
            acc = far(phase, half)
            total = acc if total is None else [x + y for x, y in zip(total, acc)]
        all_of(phase, 3).wait_recv()
        got = [give[phase, 4, i] for i in range(4)]
        for d in range(9):
            if d != 4:
                got = [got[i] + given[phase, d, i] for i in range(4)]
        v = []
        for c in range(3):
            fars = [jnp.sum(total[4 * c + t], axis=0, keepdims=True) for t in range(BLK)]
            near_c = (p[c] - (centre_x if c == 0 else 4.0)) * got[3] - got[c]
            v.append(mob_rows[...] * (far_scale * jnp.concatenate(fars, axis=0) + near_c))
        return v

    def publish(phase, p):
        for b in range(BLK):
            tile = jnp.concatenate(
                [x[b : b + 1] for x in p] + [bur_tiles[b], jnp.zeros((2, LANES), F32)], axis=0
            )
            own[phase, b] = tile
            window[phase, OWN + b] = tile
        for c in range(3):
            far_buf[c] = p[c]
        local_moments(phase)

    first_p = [pos_rows[c] for c in range(3)]
    publish(0, first_p)
    pl.semaphore_wait(barrier, n_dom - 1 + n_slab - 1 + 4)
    start_halo(0)
    start_dom(0)
    all_of(0, 0).wait_recv()
    first_v = speed(0)
    second_p = [p + time_increment * v for p, v in zip(first_p, first_v)]
    publish(1, second_p)
    start_halo(1)
    start_dom(1)
    all_of(1, 0).wait_recv()
    second_v = speed(1)
    for c in range(3):
        both = first_v[c] + second_v[c]
        for b in range(BLK):
            out_ref[c : c + 1, b * LANES : (b + 1) * LANES] = both[b : b + 1]
    for phase in range(2):
        for kind in range(4):
            all_of(phase, kind).wait_send()


def solution(mesh):
    n_slab = mesh.shape["slab"]
    n_dom = mesh.shape["dom"]

    def body(positions, burgers, mobility, block_cells, pairs, pair_count):
        segs = positions.shape[1]
        far_scale = math.sqrt(16 * n_slab / (segs * n_slab * n_dom))
        vmem = pl.BlockSpec(memory_space=pltpu.VMEM)
        smem = pl.BlockSpec(memory_space=pltpu.SMEM)
        total = pl.pallas_call(
            functools.partial(step_kernel, n_slab, n_dom, far_scale),
            out_shape=jax.ShapeDtypeStruct((3, segs), F32),
            in_specs=[vmem, vmem, vmem, smem, smem, smem],
            out_specs=vmem,
            scratch_shapes=[
                pltpu.SMEM((SLOTS,), jnp.int32),
                pltpu.SMEM((SLOTS,), jnp.int32),
                pltpu.VMEM((2 * SLOTS, LANES), F32),
                pltpu.VMEM((48, 2 * SLOTS), BF16),
                pltpu.VMEM((2, BLK, 8, LANES), F32),
                pltpu.VMEM((2, 9 * BLK, 8, LANES), F32),
                pltpu.VMEM((BLK, LANES, 48), BF16),
                pltpu.VMEM((9 * BLK, 48, 2 * LANES), BF16),
                pltpu.VMEM((9 * BLK, 16, LANES), BF16),
                pltpu.VMEM((4, 2 * SLOTS, LANES), F32),
                pltpu.VMEM((2, 9, 4, BLK, LANES), F32),
                pltpu.VMEM((2, 9, 4, BLK, LANES), F32),
                pltpu.VMEM((2, n_dom, 4, LANES), F32),
                pltpu.VMEM((2, n_slab, 4, LANES), F32),
                pltpu.VMEM((11, 8, LANES), F32),
                pltpu.VMEM((11, 48, LANES), BF16),
                pltpu.VMEM((48, segs), BF16),
                pltpu.VMEM((11, LANES, segs), F32),
                pltpu.VMEM((3, BLK, LANES), F32),
                pltpu.VMEM((3, BLK, LANES), F32),
                pltpu.VMEM((BLK, LANES), F32),
                pltpu.SemaphoreType.DMA((2, 4)),
                pltpu.SemaphoreType.DMA((2, 4)),
            ],
            compiler_params=pltpu.CompilerParams(collective_id=0, has_side_effects=True),
        )(positions, burgers, mobility.reshape(1, -1), block_cells, pairs.reshape(-1), pair_count)
        return (positions + 0.5 * time_increment * total, 0.5 * total)

    placed = (
        P(None, ("slab", "dom")),
        P(None, ("slab", "dom")),
        P(("slab", "dom")),
        P(("slab", "dom")),
        P(("slab", "dom"), None),
        P(("slab", "dom")),
    )
    return jax.shard_map(
        body,
        mesh=mesh,
        in_specs=placed,
        out_specs=(P(None, ("slab", "dom")), P(None, ("slab", "dom"))),
        check_vma=False,
    )
```

```python
import functools
import math

import jax
import jax.numpy as jnp
from jax import lax
from jax.experimental import pallas as pl
from jax.experimental.pallas import tpu as pltpu
from jax.sharding import PartitionSpec as P

MESH = pl.DeviceIdType.MESH
F32 = jnp.float32
BF16 = jnp.bfloat16

BLK = 4
LANES = 128
SLOTS = 64
OWN = 16
UNROLL = 8
FIRST_PART = 24
core_far = 9.0
time_increment = 0.25
around = [(ds, de) for ds in (-1, 0, 1) for de in (-1, 0, 1) if (ds, de) != (0, 0)]


def split3(x):
    hi = x.astype(BF16).astype(F32)
    rest = x - hi
    mid = rest.astype(BF16).astype(F32)
    return hi, mid, rest - mid


def left_stack(parts):
    hi, mid, lo = parts
    return jnp.concatenate([hi, hi, mid, hi, mid, lo], axis=0)


def right_stack(parts):
    hi, mid, lo = parts
    return jnp.concatenate([hi, mid, hi, lo, mid, hi], axis=0)


def mm(a, b, ca=1, cb=0):
    return lax.dot_general(a, b, (((ca,), (cb,)), ((), ())), preferred_element_type=F32)


def iotas():
    row = lax.broadcasted_iota(jnp.int32, (8, LANES), 0)
    lane = lax.broadcasted_iota(jnp.int32, (8, LANES), 1)
    return row, lane


def step_kernel(
    n_slab,
    n_dom,
    far_scale,
    pos_ref,
    bur_ref,
    mob_ref,
    cells_ref,
    pairs_ref,
    count_ref,
    out_ref,
    idx_a,
    idx_b,
    onehot,
    onehot_t,
    own,
    window,
    own_next,
    window_next,
    left_feat,
    right_feat,
    sums_feat,
    pair_sums,
    give,
    given,
    mom_y,
    mom_xc,
    mom_slab,
    feats,
    bur_split,
    q_buf,
    far_buf,
    pos_rows,
    mob_rows,
    send_sem,
    recv_sem,
):
    s = lax.axis_index("slab")
    e = lax.axis_index("dom")
    halves = n_slab // 8
    row, lane = iotas()
    centre_x = (4 * s + 2).astype(F32)
    centre = jnp.where(row == 0, centre_x, jnp.where(row < 3, 4.0, 0.0))

    def peer(ds, de):
        return (lax.rem(s + ds + n_slab, n_slab), lax.rem(e + de + n_dom, n_dom))

    ny = 8 if n_dom % 8 == 0 else n_dom
    nx = n_dom // ny
    nz = n_slab // 2
    x, y, z, core = e // ny, e % ny, s // 2, s % 2
    y_peers = [(s, x * ny + lax.rem(y + i, ny)) for i in range(1, ny)]
    xc_peers = [
        (2 * z + lax.rem(core + c, 2), lax.rem(x + i, nx) * ny + y)
        for i in range(nx)
        for c in range(2)
        if (i, c) != (0, 0)
    ]
    z_peers = [(2 * lax.rem(z + i, nz) + core, e) for i in range(1, nz)]

    barrier = pltpu.get_barrier_semaphore()

    def greet(slab, dom):
        pl.semaphore_signal(barrier, inc=1, device_id=(slab, dom), device_id_type=MESH)

    for group in (y_peers, xc_peers, z_peers):
        for slab, dom in group:
            greet(slab, dom)
    for ds, de in around:
        greet(*peer(ds, de))

    device = s * n_dom + e
    used = count_ref[0]

    def place(t, c):
        first = pairs_ref[0, t]
        second = pairs_ref[1, t]
        owner = second // BLK
        row_off = owner // n_dom - s + 1
        col_off = owner % n_dom - e + 1
        ia = jnp.clip(first - device * BLK, 0, BLK - 1)
        ib = jnp.clip((row_off * 3 + col_off) * BLK + second % BLK, 0, 9 * BLK - 1)
        idx_a[t] = ia
        idx_b[t] = ib
        live = t < used
        to_a = jnp.where(live, OWN + ia, LANES - 1)
        to_b = jnp.where(live, ib, LANES - 1)
        one_lane = lax.broadcasted_iota(jnp.int32, (1, LANES), 1)
        onehot[pl.ds(t, 1), :] = jnp.where(one_lane == to_a, 1.0, 0.0)
        onehot[pl.ds(SLOTS + t, 1), :] = jnp.where(one_lane == to_b, 1.0, 0.0)
        return c

    lax.fori_loop(0, SLOTS, place, 0)
    onehot_t[...] = jnp.transpose(onehot[...])[:48].astype(BF16)

    bur_tiles = []
    for b in range(BLK):
        cols = slice(b * LANES, (b + 1) * LANES)
        bur = bur_ref[:, cols]
        bur_tiles.append(bur)
        for c in range(3):
            pos_rows[c, b : b + 1, :] = pos_ref[c : c + 1, cols]
        mob_rows[b : b + 1, :] = mob_ref[:, cols]
        padded = jnp.concatenate([bur, jnp.zeros((5, LANES), F32)], axis=0)
        bur_split[:, cols] = right_stack(split3(padded)).astype(BF16)
    feats[...] = jnp.zeros(feats.shape, F32)

    def local_moments(phase):
        sums = [jnp.zeros((8, LANES), F32) for _ in range(4)]
        for b in range(BLK):
            tile = own[phase, b]
            inside = cells_ref[b] - 16 * s
            zy = (2 * (inside // 4) + 1).astype(F32)
            zz = (2 * (inside % 4) + 1).astype(F32)
            d0 = tile[0:1] - centre_x
            d1 = tile[1:2] - zy
            d2 = tile[2:3] - zz
            one = jnp.ones((1, LANES), F32)
            mono = jnp.concatenate([one, d0, d1, d2, d0 * d0, d1 * d1, d2 * d2, d0 * d1], axis=0)
            more = jnp.concatenate([d0 * d2, d1 * d2, jnp.zeros((6, LANES), F32)], axis=0)
            spot = lane == 16 * row + inside
            for k in range(3):
                bk = tile[3 + k : 4 + k]
                m = jnp.sum(mono * bk, axis=1, keepdims=True)
                sums[k] = sums[k] + jnp.where(spot, m, 0.0)
                m = jnp.sum(more * bk, axis=1, keepdims=True)
                sums[3] = sums[3] + jnp.where(lane == 16 * (row + 2 * k) + inside, m, 0.0)
        rows = [jnp.sum(x, axis=0, keepdims=True) for x in sums]
        mom_y[phase, y] = jnp.concatenate(rows, axis=0)

    def remote(src, dst, phase, kind, target):
        return pltpu.make_async_remote_copy(
            src_ref=src,
            dst_ref=dst,
            send_sem=send_sem.at[phase, kind],
            recv_sem=recv_sem.at[phase, kind],
            device_id=target,
            device_id_type=MESH,
        )

    def start_halo(phase):
        for ds, de in around:
            slot = (1 - ds) * 3 + (1 - de)
            if phase == 0:
                src, dst = own.at[0], window.at[pl.ds(slot * BLK, BLK)]
            else:
                src, dst = own_next, window_next.at[pl.ds(slot * 2, 2)]
            remote(src, dst, phase, 0, peer(ds, de)).start()

    def start_y(phase):
        mine = mom_y.at[phase, y]
        for target in y_peers:
            remote(mine, mine, phase, 1, target).start()

    def start_xc(phase):
        all_of(phase, 1).wait_recv()
        mom_xc[phase, 2 * x + core] = jnp.sum(mom_y[phase], axis=0)
        mine = mom_xc.at[phase, 2 * x + core]
        for target in xc_peers:
            remote(mine, mine, phase, 2, target).start()

    def start_z(phase):
        all_of(phase, 2).wait_recv()
        for c in range(2):
            parts = [mom_xc[phase, 2 * i + c] for i in range(nx)]
            mom_slab[phase, 2 * z + c] = sum(parts[1:], parts[0])
        mine = mom_slab.at[phase, pl.ds(2 * z, 2)]
        for target in z_peers:
            remote(mine, mine, phase, 3, target).start()

    def start_give(phase):
        for ds, de in around:
            d = (ds + 1) * 3 + de + 1
            remote(give.at[phase, d], given.at[phase, 8 - d], phase, 4, peer(ds, de)).start()

    def extent(phase, kind):
        return (
            window.at[pl.ds(0, 8 * BLK)] if phase == 0 else window_next.at[pl.ds(0, 16)],
            mom_y.at[phase, pl.ds(0, ny - 1)],
            mom_xc.at[phase, pl.ds(0, 2 * nx - 1)],
            mom_slab.at[phase, pl.ds(0, 2 * (nz - 1))],
            given.at[phase, pl.ds(0, 8)],
        )[kind]

    def all_of(phase, kind):
        whole = extent(phase, kind)
        return remote(whole, whole, phase, kind, peer(0, 1))

    def prepare(phase):
        def block(w, tile):
            r = tile - centre
            n = jnp.sum(jnp.where(row < 3, r * r, 0.0), axis=0, keepdims=True)
            mixed = jnp.where(row < 6, r, jnp.where(row == 6, n, 1.0))
            hi, mid, lo = split3(mixed)
            other = jnp.where(
                row < 3, -2.0 * r, jnp.where(row == 7, n + 0.25, jnp.where(row == 6, 1.0, 0.0))
            )
            right_feat[w, :, 0:LANES] = right_stack(split3(other)).astype(BF16)
            if phase == 0:
                is_b = (row >= 3) & (row < 6)
                bs = [jnp.where(is_b, part, 0.0) for part in (hi, mid, lo)]
                right_feat[w, :, LANES : 2 * LANES] = right_stack(bs).astype(BF16)
            sums_feat[w] = jnp.concatenate([hi, mid], axis=0).astype(BF16)

        def two(i, c):
            if phase == 0:
                first, second = window[2 * i], window[2 * i + 1]
            else:
                first = window_next[i]
                second = pltpu.roll(first, 4, 0)
            block(2 * i, first)
            block(2 * i + 1, second)
            return c

        lax.fori_loop(0, 9 * BLK // 2, two, 0)
        for b in range(BLK):
            r = own[phase, b] - centre
            n = jnp.sum(jnp.where(row < 3, r * r, 0.0), axis=0, keepdims=True)
            mixed = jnp.where(row < 6, r, jnp.where(row == 6, n, 1.0))
            left_feat[b] = jnp.transpose(left_stack(split3(mixed))).astype(BF16)

    def near(begin, end):
        def pair(t):
            ia = idx_a[t]
            ib = idx_b[t]
            both = mm(left_feat[ia], right_feat[ib])
            close = both[:, 0:LANES]
            coef = both[:, LANES : 2 * LANES]
            r1 = lax.rsqrt(close)
            r2 = lax.rsqrt(close + (core_far - 0.25))
            w = coef * (r1 * r1 * r1 - r2 * r2 * r2)
            hi = w.astype(BF16)
            lo = (w - hi.astype(F32)).astype(BF16)
            fa = sums_feat[OWN + ia]
            fb = sums_feat[ib]
            for_b = jnp.concatenate([hi, lo], axis=0)
            for_a = jnp.concatenate([jnp.transpose(hi), jnp.transpose(lo)], axis=0)
            on_b = mm(jnp.concatenate([fa, fa], axis=1), for_b)
            on_a = mm(jnp.concatenate([fb, fb], axis=1), for_a)
            on_a = on_a[0:8] + on_a[8:16]
            on_b = on_b[0:8] + on_b[8:16]
            for i, r in enumerate((0, 1, 2, 7)):
                pair_sums[i, pl.ds(t, 1), :] = on_a[r : r + 1]
                pair_sums[i, pl.ds(SLOTS + t, 1), :] = on_b[r : r + 1]

        def turn(i, c):
            for u in range(UNROLL):
                pair(i * UNROLL + u)
            return c

        lax.fori_loop(begin // UNROLL, end // UNROLL, turn, 0)

    def collect(phase):
        chosen = onehot_t[...]
        acc = []
        for i in range(4):
            hi, mid, lo = split3(pair_sums[i])
            acc.append(mm(chosen, hi.astype(BF16)) + mm(chosen, mid.astype(BF16)) + mm(chosen, lo.astype(BF16)))
        blocks = lax.broadcasted_iota(jnp.int32, (48, LANES), 0)
        shift = (4 * (1 - blocks // 12)).astype(F32)
        acc[0] = acc[0] + shift * acc[3]
        for d in range(9):
            for i in range(4):
                give[phase, d, i] = acc[i][d * BLK : (d + 1) * BLK]

    def swap_groups(m):
        for d in (1, 2, 4):
            up = pltpu.roll(pltpu.roll(m, 8 - d, 0), 16 * d, 1)
            down = pltpu.roll(pltpu.roll(m, d, 0), LANES - 16 * d, 1)
            rbit = (row // d) % 2
            gbit = (lane // (16 * d)) % 2
            m = jnp.where(rbit == gbit, m, jnp.where(rbit == 0, up, down))
        return m

    def far(phase, half):
        for q in range(4):
            rows = jnp.concatenate(
                [mom_slab[phase, half * 8 + j, q : q + 1, :] for j in range(8)], axis=0
            )
            m = swap_groups(rows)
            if q < 3:
                for f in range(8):
                    feats[f, q : q + 1, :] = m[f : f + 1] * (1.0 if f < 4 else 3.0)
                feats[10, q : q + 1, :] = -1.5 * (m[4:5] + m[5:6] + m[6:7])
            else:
                for k in range(3):
                    for f in (8, 9):
                        j = 2 * k + f - 8
                        feats[f, k : k + 1, :] = m[j : j + 1] * 3.0
        for f in range(11):
            stacked = left_stack(split3(feats[f])).astype(BF16)
            q_buf[f] = mm(stacked, bur_split[...], 0, 0)

        zz = (2 * (row % 4) + 1).astype(F32)

        def group(g, acc):
            acc = list(acc)
            zx = (4 * (half * 8 + g // 2) + 2).astype(F32)
            zy = (2 * (2 * (g % 2) + row // 4) + 1).astype(F32)
            for t in range(BLK):
                cols = slice(t * LANES, (t + 1) * LANES)
                q = [q_buf[f, pl.ds(pl.multiple_of(8 * g, 8), 8), cols] for f in range(11)]
                dx = jnp.broadcast_to(far_buf[0, t : t + 1, :] - zx, (8, LANES))
                dy = far_buf[1, t : t + 1, :] - zy
                dz = far_buf[2, t : t + 1, :] - zz
                rs = lax.rsqrt(dx * dx + (dy * dy + dz * dz + core_far))
                i2 = rs * rs
                i3 = rs * i2
                qr = q[1] * dx + q[2] * dy + q[3] * dz
                tx = q[4] * dx + q[7] * dy + q[8] * dz
                ty = q[7] * dx + q[5] * dy + q[9] * dz
                tz = q[8] * dx + q[9] * dy + q[6] * dz
                rqr = tx * dx + ty * dy + tz * dz
                scal = q[0] + i2 * (3.0 * qr + q[10] + 2.5 * i2 * rqr)
                acc[t] = acc[t] + i3 * (dx * scal - q[1] - i2 * tx)
                acc[4 + t] = acc[4 + t] + i3 * (dy * scal - q[2] - i2 * ty)
                acc[8 + t] = acc[8 + t] + i3 * (dz * scal - q[3] - i2 * tz)
            return tuple(acc)

        zero = jnp.zeros((8, LANES), F32)
        return lax.fori_loop(0, 16, group, (zero,) * 12)

    def speed(phase):
        p = [far_buf[c] for c in range(3)]
        start_xc(phase)
        all_of(phase, 0).wait_recv()
        prepare(phase)
        near(0, FIRST_PART)
        start_z(phase)
        near(FIRST_PART, SLOTS)
        collect(phase)
        start_give(phase)
        all_of(phase, 3).wait_recv()
        total = None
        for half in range(halves):
            acc = far(phase, half)
            total = acc if total is None else [u + w for u, w in zip(total, acc)]
        all_of(phase, 4).wait_recv()
        got = [give[phase, 4, i] for i in range(4)]
        for d in range(9):
            if d != 4:
                got = [got[i] + given[phase, d, i] for i in range(4)]
        v = []
        for c in range(3):
            fars = [jnp.sum(total[4 * c + t], axis=0, keepdims=True) for t in range(BLK)]
            near_c = (p[c] - (centre_x if c == 0 else 4.0)) * got[3] - got[c]
            v.append(mob_rows[...] * (far_scale * jnp.concatenate(fars, axis=0) + near_c))
        return v

    def publish(phase, p):
        for b in range(BLK):
            tile = jnp.concatenate(
                [q[b : b + 1] for q in p] + [bur_tiles[b], jnp.zeros((2, LANES), F32)], axis=0
            )
            own[phase, b] = tile
            if phase == 0:
                window[OWN + b] = tile
        if phase == 1:
            blank = jnp.zeros((1, LANES), F32)
            for half in range(2):
                rows = []
                for b in (2 * half, 2 * half + 1):
                    rows += [q[b : b + 1] for q in p] + [blank]
                packed = jnp.concatenate(rows, axis=0)
                own_next[half] = packed
                window_next[OWN // 2 + half] = packed
        for c in range(3):
            far_buf[c] = p[c]
        local_moments(phase)

    first_p = [pos_rows[c] for c in range(3)]
    publish(0, first_p)
    pl.semaphore_wait(barrier, len(y_peers) + len(xc_peers) + len(z_peers) + len(around))
    start_y(0)
    start_halo(0)
    first_v = speed(0)
    second_p = [p + time_increment * v for p, v in zip(first_p, first_v)]
    publish(1, second_p)
    start_y(1)
    start_halo(1)
    second_v = speed(1)
    for c in range(3):
        both = first_v[c] + second_v[c]
        for b in range(BLK):
            out_ref[c : c + 1, b * LANES : (b + 1) * LANES] = both[b : b + 1]
    for phase in range(2):
        for kind in range(5):
            all_of(phase, kind).wait_send()


def solution(mesh):
    n_slab = mesh.shape["slab"]
    n_dom = mesh.shape["dom"]

    def body(positions, burgers, mobility, block_cells, pairs, pair_count):
        segs = positions.shape[1]
        far_scale = math.sqrt(16 * n_slab / (segs * n_slab * n_dom))
        vmem = pl.BlockSpec(memory_space=pltpu.VMEM)
        smem = pl.BlockSpec(memory_space=pltpu.SMEM)
        total = pl.pallas_call(
            functools.partial(step_kernel, n_slab, n_dom, far_scale),
            out_shape=jax.ShapeDtypeStruct((3, segs), F32),
            in_specs=[vmem, vmem, vmem, smem, smem, smem],
            out_specs=vmem,
            scratch_shapes=[
                pltpu.SMEM((SLOTS,), jnp.int32),
                pltpu.SMEM((SLOTS,), jnp.int32),
                pltpu.VMEM((2 * SLOTS, LANES), F32),
                pltpu.VMEM((48, 2 * SLOTS), BF16),
                pltpu.VMEM((2, BLK, 8, LANES), F32),
                pltpu.VMEM((9 * BLK, 8, LANES), F32),
                pltpu.VMEM((2, 8, LANES), F32),
                pltpu.VMEM((18, 8, LANES), F32),
                pltpu.VMEM((BLK, LANES, 48), BF16),
                pltpu.VMEM((9 * BLK, 48, 2 * LANES), BF16),
                pltpu.VMEM((9 * BLK, 16, LANES), BF16),
                pltpu.VMEM((4, 2 * SLOTS, LANES), F32),
                pltpu.VMEM((2, 9, 4, BLK, LANES), F32),
                pltpu.VMEM((2, 9, 4, BLK, LANES), F32),
                pltpu.VMEM((2, 8 if n_dom % 8 == 0 else n_dom, 4, LANES), F32),
                pltpu.VMEM((2, 2 * (n_dom // 8 if n_dom % 8 == 0 else 1), 4, LANES), F32),
                pltpu.VMEM((2, n_slab, 4, LANES), F32),
                pltpu.VMEM((11, 8, LANES), F32),
                pltpu.VMEM((48, segs), BF16),
                pltpu.VMEM((11, LANES, segs), F32),
                pltpu.VMEM((3, BLK, LANES), F32),
                pltpu.VMEM((3, BLK, LANES), F32),
                pltpu.VMEM((BLK, LANES), F32),
                pltpu.SemaphoreType.DMA((2, 5)),
                pltpu.SemaphoreType.DMA((2, 5)),
            ],
            compiler_params=pltpu.CompilerParams(collective_id=0, has_side_effects=True),
        )(positions, burgers, mobility.reshape(1, -1), block_cells, pairs.T, pair_count)
        return (positions + 0.5 * time_increment * total, 0.5 * total)

    placed = (
        P(None, ("slab", "dom")),
        P(None, ("slab", "dom")),
        P(("slab", "dom")),
        P(("slab", "dom")),
        P(("slab", "dom"), None),
        P(("slab", "dom")),
    )
    return jax.shard_map(
        body,
        mesh=mesh,
        in_specs=placed,
        out_specs=(P(None, ("slab", "dom")), P(None, ("slab", "dom"))),
        check_vma=False,
    )
```

```python
import functools
import math

import jax
import jax.numpy as jnp
from jax import lax
from jax.experimental import pallas as pl
from jax.experimental.pallas import tpu as pltpu
from jax.sharding import PartitionSpec as P

MESH = pl.DeviceIdType.MESH
F32 = jnp.float32
BF16 = jnp.bfloat16

BLK = 4
LANES = 128
SLOTS = 64
OWN = 16
UNROLL = 16
FIRST_PART = 48
FAR_UNROLL = 8
core_far = 9.0
time_increment = 0.25
around = [(ds, de) for ds in (-1, 0, 1) for de in (-1, 0, 1) if (ds, de) != (0, 0)]


def split3(x):
    hi = x.astype(BF16).astype(F32)
    rest = x - hi
    mid = rest.astype(BF16).astype(F32)
    return hi, mid, rest - mid


def left_stack(parts):
    hi, mid, lo = parts
    return jnp.concatenate([hi, hi, mid, hi, mid, lo], axis=0)


def right_stack(parts):
    hi, mid, lo = parts
    return jnp.concatenate([hi, mid, hi, lo, mid, hi], axis=0)


def mm(a, b, ca=1, cb=0):
    return lax.dot_general(a, b, (((ca,), (cb,)), ((), ())), preferred_element_type=F32)


def iotas():
    row = lax.broadcasted_iota(jnp.int32, (8, LANES), 0)
    lane = lax.broadcasted_iota(jnp.int32, (8, LANES), 1)
    return row, lane


def step_kernel(
    n_slab,
    n_dom,
    far_scale,
    pos_ref,
    bur_ref,
    mob_ref,
    cells_ref,
    pairs_ref,
    count_ref,
    out_ref,
    idx_a,
    idx_b,
    onehot,
    onehot_t,
    own,
    window,
    own_next,
    window_next,
    left_feat,
    right_feat,
    sums_feat,
    pair_sums,
    give,
    given,
    mom_y,
    mom_xc,
    mom_slab,
    bur_split,
    far_buf,
    far_geo,
    pos_rows,
    mob_rows,
    send_sem,
    recv_sem,
):
    s = lax.axis_index("slab")
    e = lax.axis_index("dom")
    row, lane = iotas()
    centre_x = (4 * s + 2).astype(F32)
    centre = jnp.where(row == 0, centre_x, jnp.where(row < 3, 4.0, 0.0))

    def peer(ds, de):
        return (lax.rem(s + ds + n_slab, n_slab), lax.rem(e + de + n_dom, n_dom))

    ny = 8 if n_dom % 8 == 0 else n_dom
    nx = n_dom // ny
    nz = n_slab // 2
    x, y, z, core = e // ny, e % ny, s // 2, s % 2
    y_peers = [(s, x * ny + lax.rem(y + i, ny)) for i in range(1, ny)]
    xc_peers = [
        (2 * z + lax.rem(core + c, 2), lax.rem(x + i, nx) * ny + y)
        for i in range(nx)
        for c in range(2)
        if (i, c) != (0, 0)
    ]
    z_peers = [(2 * lax.rem(z + i, nz) + core, e) for i in range(1, nz)]

    barrier = pltpu.get_barrier_semaphore()

    def greet(slab, dom):
        pl.semaphore_signal(barrier, inc=1, device_id=(slab, dom), device_id_type=MESH)

    for group in (y_peers, xc_peers, z_peers):
        for slab, dom in group:
            greet(slab, dom)
    for ds, de in around:
        greet(*peer(ds, de))

    device = s * n_dom + e
    used = count_ref[0]

    def place(t, c):
        first = pairs_ref[0, t]
        second = pairs_ref[1, t]
        owner = second // BLK
        row_off = owner // n_dom - s + 1
        col_off = owner % n_dom - e + 1
        ia = jnp.clip(first - device * BLK, 0, BLK - 1)
        ib = jnp.clip((row_off * 3 + col_off) * BLK + second % BLK, 0, 9 * BLK - 1)
        idx_a[t] = ia
        idx_b[t] = ib
        live = t < used
        to_a = jnp.where(live, OWN + ia, LANES - 1)
        to_b = jnp.where(live, ib, LANES - 1)
        one_lane = lax.broadcasted_iota(jnp.int32, (1, LANES), 1)
        onehot[pl.ds(t, 1), :] = jnp.where(one_lane == to_a, 1.0, 0.0)
        onehot[pl.ds(SLOTS + t, 1), :] = jnp.where(one_lane == to_b, 1.0, 0.0)
        return c

    bur_tiles = []
    for b in range(BLK):
        cols = slice(b * LANES, (b + 1) * LANES)
        bur = bur_ref[:, cols]
        bur_tiles.append(bur)
        for c in range(3):
            pos_rows[c, b : b + 1, :] = pos_ref[c : c + 1, cols]
        mob_rows[b : b + 1, :] = mob_ref[:, cols]

    def set_up():
        lax.fori_loop(0, SLOTS, place, 0)
        onehot_t[...] = jnp.transpose(onehot[...])[:48].astype(BF16)
        blank = jnp.zeros((3, LANES), F32)
        for b, bur in enumerate(bur_tiles):
            cols = slice(b * LANES, (b + 1) * LANES)
            upper = jnp.concatenate([bur, blank, blank[0:2]], axis=0)
            lower = jnp.concatenate([blank, bur, blank[0:2]], axis=0)
            bur_split[0, :, cols] = right_stack(split3(upper)).astype(BF16)
            bur_split[1, :, cols] = right_stack(split3(lower)).astype(BF16)

    def local_moments(phase):
        sums = [jnp.zeros((8, LANES), F32) for _ in range(6)]
        for b in range(BLK):
            tile = own[phase, b]
            inside = cells_ref[b] - 16 * s
            zy = (2 * (inside // 4) + 1).astype(F32)
            zz = (2 * (inside % 4) + 1).astype(F32)
            d0 = tile[0:1] - centre_x
            d1 = tile[1:2] - zy
            d2 = tile[2:3] - zz
            one = jnp.ones((1, LANES), F32)
            squares = [3.0 * d * d for d in (d0, d1, d2)]
            mono = jnp.concatenate([one, d0, d1, d2, *squares, 3.0 * d0 * d1], axis=0)
            trace = -0.5 * (squares[0] + squares[1] + squares[2])
            more = jnp.concatenate(
                [3.0 * d0 * d2, 3.0 * d1 * d2, trace, jnp.zeros((5, LANES), F32)], axis=0
            )
            spot = lane == 16 * row + inside
            for k in range(3):
                bk = tile[3 + k : 4 + k]
                m = jnp.sum(mono * bk, axis=1, keepdims=True)
                sums[k] = sums[k] + jnp.where(spot, m, 0.0)
                m = jnp.sum(more * bk, axis=1, keepdims=True)
                sums[3 + k] = sums[3 + k] + jnp.where(spot, m, 0.0)
        rows = [jnp.sum(m, axis=0, keepdims=True) for m in sums]
        mom_y[phase, y] = jnp.concatenate(rows + [jnp.zeros((2, LANES), F32)], axis=0)

    def remote(src, dst, phase, kind, target):
        return pltpu.make_async_remote_copy(
            src_ref=src,
            dst_ref=dst,
            send_sem=send_sem.at[phase, kind],
            recv_sem=recv_sem.at[phase, kind],
            device_id=target,
            device_id_type=MESH,
        )

    def start_halo(phase):
        for ds, de in around:
            slot = (1 - ds) * 3 + (1 - de)
            if phase == 0:
                src, dst = own.at[0], window.at[pl.ds(slot * BLK, BLK)]
            else:
                src, dst = own_next, window_next.at[pl.ds(slot * 2, 2)]
            remote(src, dst, phase, 0, peer(ds, de)).start()

    def start_y(phase):
        mine = mom_y.at[phase, y]
        for target in y_peers:
            remote(mine, mine, phase, 1, target).start()

    def start_xc(phase):
        all_of(phase, 1).wait_recv()
        mom_xc[phase, 2 * x + core] = jnp.sum(mom_y[phase], axis=0)
        mine = mom_xc.at[phase, 2 * x + core]
        for target in xc_peers:
            remote(mine, mine, phase, 2, target).start()

    def start_z(phase):
        all_of(phase, 2).wait_recv()
        for c in range(2):
            parts = [mom_xc[phase, 2 * i + c] for i in range(nx)]
            mom_slab[phase, 2 * z + c] = sum(parts[1:], parts[0])
        mine = mom_slab.at[phase, pl.ds(2 * z, 2)]
        for target in z_peers:
            remote(mine, mine, phase, 3, target).start()

    def start_give(phase):
        for ds, de in around:
            d = (ds + 1) * 3 + de + 1
            remote(give.at[phase, d], given.at[phase, 8 - d], phase, 4, peer(ds, de)).start()

    def extent(phase, kind):
        return (
            window.at[pl.ds(0, 8 * BLK)] if phase == 0 else window_next.at[pl.ds(0, 16)],
            mom_y.at[phase, pl.ds(0, ny - 1)],
            mom_xc.at[phase, pl.ds(0, 2 * nx - 1)],
            mom_slab.at[phase, pl.ds(0, 2 * (nz - 1))],
            given.at[phase, pl.ds(0, 8)],
        )[kind]

    def all_of(phase, kind):
        whole = extent(phase, kind)
        return remote(whole, whole, phase, kind, peer(0, 1))

    def prepare(phase):
        def block(w, tile):
            r = tile - centre
            n = jnp.sum(jnp.where(row < 3, r * r, 0.0), axis=0, keepdims=True)
            mixed = jnp.where(row < 6, r, jnp.where(row == 6, n, 1.0))
            hi, mid, lo = split3(mixed)
            other = jnp.where(
                row < 3, -2.0 * r, jnp.where(row == 7, n + 0.25, jnp.where(row == 6, 1.0, 0.0))
            )
            right_feat[w, :, 0:LANES] = right_stack(split3(other)).astype(BF16)
            if phase == 0:
                is_b = (row >= 3) & (row < 6)
                bs = [jnp.where(is_b, part, 0.0) for part in (hi, mid, lo)]
                right_feat[w, :, LANES : 2 * LANES] = right_stack(bs).astype(BF16)
            sums_feat[w] = jnp.concatenate([hi, mid], axis=0).astype(BF16)

        def two(i, c):
            if phase == 0:
                first, second = window[2 * i], window[2 * i + 1]
            else:
                first = window_next[i]
                second = pltpu.roll(first, 4, 0)
            block(2 * i, first)
            block(2 * i + 1, second)
            return c

        lax.fori_loop(0, 9 * BLK // 2, two, 0)

    def prepare_own(phase, p):
        for c in range(3):
            far_buf[c] = p[c]
        for b in range(BLK):
            tile = own[phase, b]
            if phase == 0:
                window[OWN + b] = tile
        for half in range(2):
            if phase == 1:
                window_next[OWN // 2 + half] = own_next[half]
        zz = (2 * (row % 4) + 1).astype(F32)
        for t in range(BLK):
            dz = p[2][t : t + 1] - zz
            far_geo[2, t] = dz
            for par in range(2):
                dy = p[1][t : t + 1] - (2 * (2 * par + row // 4) + 1).astype(F32)
                far_geo[par, t] = dy
                far_geo[3 + par, t] = dy * dy + dz * dz + core_far
        for b in range(BLK):
            r = own[phase, b] - centre
            n = jnp.sum(jnp.where(row < 3, r * r, 0.0), axis=0, keepdims=True)
            mixed = jnp.where(row < 6, r, jnp.where(row == 6, n, 1.0))
            left_feat[b] = jnp.transpose(left_stack(split3(mixed))).astype(BF16)

    def near(begin, end):
        def pair(t):
            ia = idx_a[t]
            ib = idx_b[t]
            both = mm(left_feat[ia], right_feat[ib])
            close = both[:, 0:LANES]
            coef = both[:, LANES : 2 * LANES]
            r1 = lax.rsqrt(close)
            r2 = lax.rsqrt(close + (core_far - 0.25))
            w = coef * (r1 * r1 * r1 - r2 * r2 * r2)
            hi = w.astype(BF16)
            lo = (w - hi.astype(F32)).astype(BF16)
            fa = sums_feat[OWN + ia]
            fb = sums_feat[ib]
            for_b = jnp.concatenate([hi, lo], axis=0)
            for_a = jnp.concatenate([jnp.transpose(hi), jnp.transpose(lo)], axis=0)
            on_b = mm(jnp.concatenate([fa, fa], axis=1), for_b)
            on_a = mm(jnp.concatenate([fb, fb], axis=1), for_a)
            on_a = on_a[0:8] + on_a[8:16]
            on_b = on_b[0:8] + on_b[8:16]
            for i, r in enumerate((0, 1, 2, 7)):
                pair_sums[i, pl.ds(t, 1), :] = on_a[r : r + 1]
                pair_sums[i, pl.ds(SLOTS + t, 1), :] = on_b[r : r + 1]

        def turn(i, c):
            for u in range(UNROLL):
                pair(i * UNROLL + u)
            return c

        lax.fori_loop(begin // UNROLL, end // UNROLL, turn, 0)

    def collect(phase):
        chosen = onehot_t[...]
        acc = []
        for i in range(4):
            hi, mid, lo = split3(pair_sums[i])
            acc.append(mm(chosen, hi.astype(BF16)) + mm(chosen, mid.astype(BF16)) + mm(chosen, lo.astype(BF16)))
        blocks = lax.broadcasted_iota(jnp.int32, (48, LANES), 0)
        shift = (4 * (1 - blocks // 12)).astype(F32)
        acc[0] = acc[0] + shift * acc[3]
        for d in range(9):
            for i in range(4):
                give[phase, d, i] = acc[i][d * BLK : (d + 1) * BLK]

    def far(phase):
        def products(j):
            stacked = jnp.transpose(left_stack(split3(mom_slab[phase, j]))).astype(BF16)
            return mm(stacked, bur_split[0]), mm(stacked[0:48], bur_split[1])

        def forces(j, found, acc):
            q1, q2 = found
            zx = (4 * j + 2).astype(F32)
            for t in range(BLK):
                cols = slice(t * LANES, (t + 1) * LANES)
                dx = jnp.broadcast_to(far_buf[0, t : t + 1, :] - zx, (8, LANES))
                dx2 = dx * dx
                dz = far_geo[2, t]
                for par in range(2):
                    q = [q1[16 * f + 8 * par : 16 * f + 8 * par + 8, cols] for f in range(8)]
                    q += [q2[16 * f + 8 * par : 16 * f + 8 * par + 8, cols] for f in range(3)]
                    dy = far_geo[par, t]
                    rs = lax.rsqrt(dx2 + far_geo[3 + par, t])
                    i2 = rs * rs
                    i3 = rs * i2
                    tx = q[4] * dx + q[7] * dy + q[8] * dz
                    ty = q[7] * dx + q[5] * dy + q[9] * dz
                    tz = q[8] * dx + q[9] * dy + q[6] * dz
                    qr = q[1] * dx + q[2] * dy + q[3] * dz
                    rqr = tx * dx + ty * dy + tz * dz
                    scal = q[0] + i2 * (3.0 * qr + q[10] + 2.5 * i2 * rqr)
                    acc[t] = acc[t] + i3 * (dx * scal - q[1] - i2 * tx)
                    acc[4 + t] = acc[4 + t] + i3 * (dy * scal - q[2] - i2 * ty)
                    acc[8 + t] = acc[8 + t] + i3 * (dz * scal - q[3] - i2 * tz)
            return acc

        def turn(i, acc):
            acc = list(acc)
            for u in range(FAR_UNROLL):
                j = FAR_UNROLL * i + u
                acc = forces(j, products(j), acc)
            return tuple(acc)

        zero = jnp.zeros((8, LANES), F32)
        return lax.fori_loop(0, n_slab // FAR_UNROLL, turn, (zero,) * 12)

    def speed(phase):
        p = [far_buf[c] for c in range(3)]
        start_xc(phase)
        all_of(phase, 0).wait_recv()
        prepare(phase)
        near(0, FIRST_PART)
        start_z(phase)
        near(FIRST_PART, SLOTS)
        collect(phase)
        start_give(phase)
        all_of(phase, 3).wait_recv()
        total = far(phase)
        all_of(phase, 4).wait_recv()
        got = [give[phase, 4, i] for i in range(4)]
        for d in range(9):
            if d != 4:
                got = [got[i] + given[phase, d, i] for i in range(4)]
        v = []
        for c in range(3):
            fars = [jnp.sum(total[4 * c + t], axis=0, keepdims=True) for t in range(BLK)]
            near_c = (p[c] - (centre_x if c == 0 else 4.0)) * got[3] - got[c]
            v.append(mob_rows[...] * (far_scale * jnp.concatenate(fars, axis=0) + near_c))
        return v

    def publish(phase, p):
        for b in range(BLK):
            own[phase, b] = jnp.concatenate(
                [q[b : b + 1] for q in p] + [bur_tiles[b], jnp.zeros((2, LANES), F32)], axis=0
            )
        if phase == 1:
            blank = jnp.zeros((1, LANES), F32)
            for half in range(2):
                rows = []
                for b in (2 * half, 2 * half + 1):
                    rows += [q[b : b + 1] for q in p] + [blank]
                own_next[half] = jnp.concatenate(rows, axis=0)
        local_moments(phase)

    first_p = [pos_rows[c] for c in range(3)]
    publish(0, first_p)
    pl.semaphore_wait(barrier, len(y_peers) + len(xc_peers) + len(z_peers) + len(around))
    start_y(0)
    start_halo(0)
    set_up()
    prepare_own(0, first_p)
    first_v = speed(0)
    second_p = [p + time_increment * v for p, v in zip(first_p, first_v)]
    publish(1, second_p)
    start_y(1)
    start_halo(1)
    prepare_own(1, second_p)
    second_v = speed(1)
    for c in range(3):
        both = first_v[c] + second_v[c]
        for b in range(BLK):
            out_ref[c : c + 1, b * LANES : (b + 1) * LANES] = both[b : b + 1]
    for phase in range(2):
        for kind in range(5):
            all_of(phase, kind).wait_send()


def solution(mesh):
    n_slab = mesh.shape["slab"]
    n_dom = mesh.shape["dom"]

    def body(positions, burgers, mobility, block_cells, pairs, pair_count):
        segs = positions.shape[1]
        far_scale = math.sqrt(16 * n_slab / (segs * n_slab * n_dom))
        vmem = pl.BlockSpec(memory_space=pltpu.VMEM)
        smem = pl.BlockSpec(memory_space=pltpu.SMEM)
        total = pl.pallas_call(
            functools.partial(step_kernel, n_slab, n_dom, far_scale),
            out_shape=jax.ShapeDtypeStruct((3, segs), F32),
            in_specs=[vmem, vmem, vmem, smem, smem, smem],
            out_specs=vmem,
            scratch_shapes=[
                pltpu.SMEM((SLOTS,), jnp.int32),
                pltpu.SMEM((SLOTS,), jnp.int32),
                pltpu.VMEM((2 * SLOTS, LANES), F32),
                pltpu.VMEM((48, 2 * SLOTS), BF16),
                pltpu.VMEM((2, BLK, 8, LANES), F32),
                pltpu.VMEM((9 * BLK, 8, LANES), F32),
                pltpu.VMEM((2, 8, LANES), F32),
                pltpu.VMEM((18, 8, LANES), F32),
                pltpu.VMEM((BLK, LANES, 48), BF16),
                pltpu.VMEM((9 * BLK, 48, 2 * LANES), BF16),
                pltpu.VMEM((9 * BLK, 16, LANES), BF16),
                pltpu.VMEM((4, 2 * SLOTS, LANES), F32),
                pltpu.VMEM((2, 9, 4, BLK, LANES), F32),
                pltpu.VMEM((2, 9, 4, BLK, LANES), F32),
                pltpu.VMEM((2, 8 if n_dom % 8 == 0 else n_dom, 8, LANES), F32),
                pltpu.VMEM((2, 2 * (n_dom // 8 if n_dom % 8 == 0 else 1), 8, LANES), F32),
                pltpu.VMEM((2, n_slab, 8, LANES), F32),
                pltpu.VMEM((2, 48, segs), BF16),
                pltpu.VMEM((3, BLK, LANES), F32),
                pltpu.VMEM((5, BLK, 8, LANES), F32),
                pltpu.VMEM((3, BLK, LANES), F32),
                pltpu.VMEM((BLK, LANES), F32),
                pltpu.SemaphoreType.DMA((2, 5)),
                pltpu.SemaphoreType.DMA((2, 5)),
            ],
            compiler_params=pltpu.CompilerParams(collective_id=0, has_side_effects=True),
        )(positions, burgers, mobility.reshape(1, -1), block_cells, pairs.T, pair_count)
        return (positions + 0.5 * time_increment * total, 0.5 * total)

    placed = (
        P(None, ("slab", "dom")),
        P(None, ("slab", "dom")),
        P(("slab", "dom")),
        P(("slab", "dom")),
        P(("slab", "dom"), None),
        P(("slab", "dom")),
    )
    return jax.shard_map(
        body,
        mesh=mesh,
        in_specs=placed,
        out_specs=(P(None, ("slab", "dom")), P(None, ("slab", "dom"))),
        check_vma=False,
    )
```

```python
import functools
import math

import jax
import jax.numpy as jnp
from jax import lax
from jax.experimental import pallas as pl
from jax.experimental.pallas import tpu as pltpu
from jax.sharding import PartitionSpec as P

MESH = pl.DeviceIdType.MESH
F32 = jnp.float32
BF16 = jnp.bfloat16

BLK = 4
LANES = 128
SLOTS = 64
OWN = 16
UNROLL = 16
FIRST_PART = 48
NEAR_Z = 2
core_far = 9.0
time_increment = 0.25
around = [(-1, -1), (-1, 1), (1, -1), (1, 1), (0, -1), (0, 1), (-1, 0), (1, 0)]


def split3(x):
    hi = x.astype(BF16).astype(F32)
    rest = x - hi
    mid = rest.astype(BF16).astype(F32)
    return hi, mid, rest - mid


def left_stack(parts):
    hi, mid, lo = parts
    return jnp.concatenate([hi, hi, mid, hi, mid, lo], axis=0)


def right_stack(parts):
    hi, mid, lo = parts
    return jnp.concatenate([hi, mid, hi, lo, mid, hi], axis=0)


def mm(a, b, ca=1, cb=0):
    return lax.dot_general(a, b, (((ca,), (cb,)), ((), ())), preferred_element_type=F32)


def iotas():
    row = lax.broadcasted_iota(jnp.int32, (8, LANES), 0)
    lane = lax.broadcasted_iota(jnp.int32, (8, LANES), 1)
    return row, lane


def step_kernel(
    n_slab,
    n_dom,
    far_scale,
    pos_ref,
    bur_ref,
    mob_ref,
    cells_ref,
    pairs_ref,
    count_ref,
    out_ref,
    idx_a,
    idx_b,
    onehot,
    onehot_t,
    own,
    window,
    own_next,
    window_next,
    left_feat,
    right_feat,
    sums_feat,
    pair_sums,
    give,
    given,
    mom_y,
    mom_xc,
    mom_slab,
    bur_split,
    far_buf,
    far_geo,
    pos_rows,
    mob_rows,
    send_sem,
    recv_sem,
):
    s = lax.axis_index("slab")
    e = lax.axis_index("dom")
    row, lane = iotas()
    centre_x = (4 * s + 2).astype(F32)
    centre = jnp.where(row == 0, centre_x, jnp.where(row < 3, 4.0, 0.0))

    def peer(ds, de):
        return (lax.rem(s + ds + n_slab, n_slab), lax.rem(e + de + n_dom, n_dom))

    ny = 8 if n_dom % 8 == 0 else n_dom
    nx = n_dom // ny
    nz = n_slab // 2
    x, y, z, core = e // ny, e % ny, s // 2, s % 2
    far_first = lambda n: sorted(range(1, n), key=lambda i: -min(i, n - i))
    y_peers = [(s, x * ny + lax.rem(y + i, ny)) for i in far_first(ny)]
    xc_peers = [
        (2 * z + lax.rem(core + c, 2), lax.rem(x + i, nx) * ny + y)
        for i in far_first(nx) + [0]
        for c in range(2)
        if (i, c) != (0, 0)
    ]
    z_peers = [(2 * lax.rem(z + i, nz) + core, e) for i in far_first(nz)]

    barrier = pltpu.get_barrier_semaphore()

    def greet(slab, dom):
        pl.semaphore_signal(barrier, inc=1, device_id=(slab, dom), device_id_type=MESH)

    for group in (y_peers, xc_peers, z_peers):
        for slab, dom in group:
            greet(slab, dom)
    for ds, de in around:
        greet(*peer(ds, de))

    device = s * n_dom + e
    used = count_ref[0]

    def place(t, c):
        first = pairs_ref[0, t]
        second = pairs_ref[1, t]
        owner = second // BLK
        row_off = owner // n_dom - s + 1
        col_off = owner % n_dom - e + 1
        ia = jnp.clip(first - device * BLK, 0, BLK - 1)
        ib = jnp.clip((row_off * 3 + col_off) * BLK + second % BLK, 0, 9 * BLK - 1)
        idx_a[t] = ia
        idx_b[t] = ib
        live = t < used
        to_a = jnp.where(live, OWN + ia, LANES - 1)
        to_b = jnp.where(live, ib, LANES - 1)
        one_lane = lax.broadcasted_iota(jnp.int32, (1, LANES), 1)
        onehot[pl.ds(t, 1), :] = jnp.where(one_lane == to_a, 1.0, 0.0)
        onehot[pl.ds(SLOTS + t, 1), :] = jnp.where(one_lane == to_b, 1.0, 0.0)
        return c

    bur_tiles = []
    for b in range(BLK):
        cols = slice(b * LANES, (b + 1) * LANES)
        bur = bur_ref[:, cols]
        bur_tiles.append(bur)
        for c in range(3):
            pos_rows[c, b : b + 1, :] = pos_ref[c : c + 1, cols]
        mob_rows[b : b + 1, :] = mob_ref[:, cols]

    def set_up():
        lax.fori_loop(0, SLOTS, place, 0)
        onehot_t[...] = jnp.transpose(onehot[...])[:48].astype(BF16)
        blank = jnp.zeros((3, LANES), F32)
        for b, bur in enumerate(bur_tiles):
            cols = slice(b * LANES, (b + 1) * LANES)
            upper = jnp.concatenate([bur, blank, blank[0:2]], axis=0)
            lower = jnp.concatenate([blank, bur, blank[0:2]], axis=0)
            bur_split[0, :, cols] = right_stack(split3(upper)).astype(BF16)
            bur_split[1, :, cols] = right_stack(split3(lower)).astype(BF16)

    def local_moments(phase):
        sums = [jnp.zeros((8, LANES), F32) for _ in range(6)]
        for b in range(BLK):
            tile = own[phase, b]
            inside = cells_ref[b] - 16 * s
            zy = (2 * (inside // 4) + 1).astype(F32)
            zz = (2 * (inside % 4) + 1).astype(F32)
            d0 = tile[0:1] - centre_x
            d1 = tile[1:2] - zy
            d2 = tile[2:3] - zz
            one = jnp.ones((1, LANES), F32)
            squares = [3.0 * d * d for d in (d0, d1, d2)]
            mono = jnp.concatenate([one, d0, d1, d2, *squares, 3.0 * d0 * d1], axis=0)
            trace = -0.5 * (squares[0] + squares[1] + squares[2])
            more = jnp.concatenate(
                [3.0 * d0 * d2, 3.0 * d1 * d2, trace, jnp.zeros((5, LANES), F32)], axis=0
            )
            spot = lane == 16 * row + inside
            for k in range(3):
                bk = tile[3 + k : 4 + k]
                m = jnp.sum(mono * bk, axis=1, keepdims=True)
                sums[k] = sums[k] + jnp.where(spot, m, 0.0)
                m = jnp.sum(more * bk, axis=1, keepdims=True)
                sums[3 + k] = sums[3 + k] + jnp.where(spot, m, 0.0)
        rows = [jnp.sum(m, axis=0, keepdims=True) for m in sums]
        mom_y[phase, y] = jnp.concatenate(rows + [jnp.zeros((2, LANES), F32)], axis=0)

    def remote(src, dst, phase, kind, target):
        return pltpu.make_async_remote_copy(
            src_ref=src,
            dst_ref=dst,
            send_sem=send_sem.at[phase, kind],
            recv_sem=recv_sem.at[phase, kind],
            device_id=target,
            device_id_type=MESH,
        )

    def start_halo(phase):
        for ds, de in around:
            slot = (1 - ds) * 3 + (1 - de)
            if phase == 0:
                src, dst = own.at[0], window.at[pl.ds(slot * BLK, BLK)]
            else:
                src, dst = own_next, window_next.at[pl.ds(slot * 2, 2)]
            remote(src, dst, phase, 0, peer(ds, de)).start()

    def start_y(phase):
        mine = mom_y.at[phase, y]
        for target in y_peers:
            remote(mine, mine, phase, 1, target).start()

    def start_xc(phase):
        all_of(phase, 1).wait_recv()
        mom_xc[phase, 2 * x + core] = jnp.sum(mom_y[phase], axis=0)
        mine = mom_xc.at[phase, 2 * x + core]
        for target in xc_peers:
            remote(mine, mine, phase, 2, target).start()

    def start_z(phase):
        all_of(phase, 2).wait_recv()
        for c in range(2):
            parts = [mom_xc[phase, 2 * i + c] for i in range(nx)]
            mom_slab[phase, 2 * z + c] = sum(parts[1:], parts[0])
        mine = mom_slab.at[phase, pl.ds(2 * z, 2)]
        for i, target in zip(far_first(nz), z_peers):
            remote(mine, mine, phase, 3 if min(i, nz - i) <= NEAR_Z else 5, target).start()

    def start_give(phase):
        for ds, de in around:
            d = (ds + 1) * 3 + de + 1
            remote(give.at[phase, d], given.at[phase, 8 - d], phase, 4, peer(ds, de)).start()

    def extent(phase, kind):
        return (
            window.at[pl.ds(0, 8 * BLK)] if phase == 0 else window_next.at[pl.ds(0, 16)],
            mom_y.at[phase, pl.ds(0, ny - 1)],
            mom_xc.at[phase, pl.ds(0, 2 * nx - 1)],
            mom_slab.at[phase, pl.ds(0, 4 * NEAR_Z)],
            given.at[phase, pl.ds(0, 8)],
            mom_slab.at[phase, pl.ds(0, 2 * (nz - 1) - 4 * NEAR_Z)],
        )[kind]

    def all_of(phase, kind):
        whole = extent(phase, kind)
        return remote(whole, whole, phase, kind, peer(0, 1))

    def prepare(phase):
        def block(w, tile):
            r = tile - centre
            n = jnp.sum(jnp.where(row < 3, r * r, 0.0), axis=0, keepdims=True)
            mixed = jnp.where(row < 6, r, jnp.where(row == 6, n, 1.0))
            hi, mid, lo = split3(mixed)
            other = jnp.where(
                row < 3, -2.0 * r, jnp.where(row == 7, n + 0.25, jnp.where(row == 6, 1.0, 0.0))
            )
            right_feat[w, :, 0:LANES] = right_stack(split3(other)).astype(BF16)
            if phase == 0:
                is_b = (row >= 3) & (row < 6)
                bs = [jnp.where(is_b, part, 0.0) for part in (hi, mid, lo)]
                right_feat[w, :, LANES : 2 * LANES] = right_stack(bs).astype(BF16)
            sums_feat[w] = jnp.concatenate([hi, mid], axis=0).astype(BF16)

        def two(i, c):
            if phase == 0:
                first, second = window[2 * i], window[2 * i + 1]
            else:
                first = window_next[i]
                second = pltpu.roll(first, 4, 0)
            block(2 * i, first)
            block(2 * i + 1, second)
            return c

        lax.fori_loop(0, 9 * BLK // 2, two, 0)

    def prepare_own(phase, p):
        for c in range(3):
            far_buf[c] = p[c]
        for b in range(BLK):
            tile = own[phase, b]
            if phase == 0:
                window[OWN + b] = tile
        for half in range(2):
            if phase == 1:
                window_next[OWN // 2 + half] = own_next[half]
        zz = (2 * (row % 4) + 1).astype(F32)
        for t in range(BLK):
            dz = p[2][t : t + 1] - zz
            far_geo[2, t] = dz
            for par in range(2):
                dy = p[1][t : t + 1] - (2 * (2 * par + row // 4) + 1).astype(F32)
                far_geo[par, t] = dy
                far_geo[3 + par, t] = dy * dy + dz * dz + core_far
        for b in range(BLK):
            r = own[phase, b] - centre
            n = jnp.sum(jnp.where(row < 3, r * r, 0.0), axis=0, keepdims=True)
            mixed = jnp.where(row < 6, r, jnp.where(row == 6, n, 1.0))
            left_feat[b] = jnp.transpose(left_stack(split3(mixed))).astype(BF16)

    def near(begin, end):
        def pair(t):
            ia = idx_a[t]
            ib = idx_b[t]
            both = mm(left_feat[ia], right_feat[ib])
            close = both[:, 0:LANES]
            coef = both[:, LANES : 2 * LANES]
            r1 = lax.rsqrt(close)
            r2 = lax.rsqrt(close + (core_far - 0.25))
            w = coef * (r1 * r1 * r1 - r2 * r2 * r2)
            hi = w.astype(BF16)
            lo = (w - hi.astype(F32)).astype(BF16)
            fa = sums_feat[OWN + ia]
            fb = sums_feat[ib]
            for_b = jnp.concatenate([hi, lo], axis=0)
            for_a = jnp.concatenate([jnp.transpose(hi), jnp.transpose(lo)], axis=0)
            on_b = mm(jnp.concatenate([fa, fa], axis=1), for_b)
            on_a = mm(jnp.concatenate([fb, fb], axis=1), for_a)
            on_a = on_a[0:8] + on_a[8:16]
            on_b = on_b[0:8] + on_b[8:16]
            for i, r in enumerate((0, 1, 2, 7)):
                pair_sums[i, pl.ds(t, 1), :] = on_a[r : r + 1]
                pair_sums[i, pl.ds(SLOTS + t, 1), :] = on_b[r : r + 1]

        def turn(i, c):
            for u in range(UNROLL):
                pair(i * UNROLL + u)
            return c

        lax.fori_loop(begin // UNROLL, end // UNROLL, turn, 0)

    def collect(phase):
        chosen = onehot_t[...]
        acc = []
        for i in range(4):
            hi, mid, lo = split3(pair_sums[i])
            acc.append(mm(chosen, hi.astype(BF16)) + mm(chosen, mid.astype(BF16)) + mm(chosen, lo.astype(BF16)))
        blocks = lax.broadcasted_iota(jnp.int32, (48, LANES), 0)
        shift = (4 * (1 - blocks // 12)).astype(F32)
        acc[0] = acc[0] + shift * acc[3]
        for d in range(9):
            for i in range(4):
                give[phase, d, i] = acc[i][d * BLK : (d + 1) * BLK]

    def far(phase, begin, end, acc):
        def products(j):
            stacked = jnp.transpose(left_stack(split3(mom_slab[phase, j]))).astype(BF16)
            return mm(stacked, bur_split[0]), mm(stacked[0:48], bur_split[1])

        def forces(j, found, acc):
            q1, q2 = found
            zx = (4 * j + 2).astype(F32)
            for t in range(BLK):
                cols = slice(t * LANES, (t + 1) * LANES)
                dx = jnp.broadcast_to(far_buf[0, t : t + 1, :] - zx, (8, LANES))
                dx2 = dx * dx
                dz = far_geo[2, t]
                for par in range(2):
                    q = [q1[16 * f + 8 * par : 16 * f + 8 * par + 8, cols] for f in range(8)]
                    q += [q2[16 * f + 8 * par : 16 * f + 8 * par + 8, cols] for f in range(3)]
                    dy = far_geo[par, t]
                    rs = lax.rsqrt(dx2 + far_geo[3 + par, t])
                    i2 = rs * rs
                    i3 = rs * i2
                    tx = q[4] * dx + q[7] * dy + q[8] * dz
                    ty = q[7] * dx + q[5] * dy + q[9] * dz
                    tz = q[8] * dx + q[9] * dy + q[6] * dz
                    qr = q[1] * dx + q[2] * dy + q[3] * dz
                    rqr = tx * dx + ty * dy + tz * dz
                    scal = q[0] + i2 * (3.0 * qr + q[10] + 2.5 * i2 * rqr)
                    acc[t] = acc[t] + i3 * (dx * scal - q[1] - i2 * tx)
                    acc[4 + t] = acc[4 + t] + i3 * (dy * scal - q[2] - i2 * ty)
                    acc[8 + t] = acc[8 + t] + i3 * (dz * scal - q[3] - i2 * tz)
            return acc

        acc = list(acc)
        for i in range(begin, end):
            j = lax.rem(2 * (z + nz - NEAR_Z) + i, n_slab)
            acc = forces(j, products(j), acc)
        return acc

    def speed(phase):
        p = [far_buf[c] for c in range(3)]
        start_xc(phase)
        all_of(phase, 0).wait_recv()
        prepare(phase)
        near(0, FIRST_PART)
        start_z(phase)
        near(FIRST_PART, SLOTS)
        collect(phase)
        start_give(phase)
        zero = jnp.zeros((8, LANES), F32)
        middle = 4 * NEAR_Z + 2
        all_of(phase, 3).wait_recv()
        total = far(phase, 0, middle, [zero] * 12)
        all_of(phase, 5).wait_recv()
        total = far(phase, middle, n_slab, total)
        all_of(phase, 4).wait_recv()
        got = [give[phase, 4, i] for i in range(4)]
        for d in range(9):
            if d != 4:
                got = [got[i] + given[phase, d, i] for i in range(4)]
        v = []
        for c in range(3):
            fars = [jnp.sum(total[4 * c + t], axis=0, keepdims=True) for t in range(BLK)]
            near_c = (p[c] - (centre_x if c == 0 else 4.0)) * got[3] - got[c]
            v.append(mob_rows[...] * (far_scale * jnp.concatenate(fars, axis=0) + near_c))
        return v

    def publish(phase, p):
        for b in range(BLK):
            own[phase, b] = jnp.concatenate(
                [q[b : b + 1] for q in p] + [bur_tiles[b], jnp.zeros((2, LANES), F32)], axis=0
            )
        if phase == 1:
            blank = jnp.zeros((1, LANES), F32)
            for half in range(2):
                rows = []
                for b in (2 * half, 2 * half + 1):
                    rows += [q[b : b + 1] for q in p] + [blank]
                own_next[half] = jnp.concatenate(rows, axis=0)
        local_moments(phase)

    first_p = [pos_rows[c] for c in range(3)]
    publish(0, first_p)
    pl.semaphore_wait(barrier, len(y_peers) + len(xc_peers) + len(z_peers) + len(around))
    start_y(0)
    start_halo(0)
    set_up()
    prepare_own(0, first_p)
    first_v = speed(0)
    second_p = [p + time_increment * v for p, v in zip(first_p, first_v)]
    publish(1, second_p)
    start_y(1)
    start_halo(1)
    prepare_own(1, second_p)
    second_v = speed(1)
    for c in range(3):
        both = first_v[c] + second_v[c]
        for b in range(BLK):
            out_ref[c : c + 1, b * LANES : (b + 1) * LANES] = both[b : b + 1]
    for phase in range(2):
        for kind in range(6):
            all_of(phase, kind).wait_send()


def solution(mesh):
    n_slab = mesh.shape["slab"]
    n_dom = mesh.shape["dom"]

    def body(positions, burgers, mobility, block_cells, pairs, pair_count):
        segs = positions.shape[1]
        far_scale = math.sqrt(16 * n_slab / (segs * n_slab * n_dom))
        vmem = pl.BlockSpec(memory_space=pltpu.VMEM)
        smem = pl.BlockSpec(memory_space=pltpu.SMEM)
        total = pl.pallas_call(
            functools.partial(step_kernel, n_slab, n_dom, far_scale),
            out_shape=jax.ShapeDtypeStruct((3, segs), F32),
            in_specs=[vmem, vmem, vmem, smem, smem, smem],
            out_specs=vmem,
            scratch_shapes=[
                pltpu.SMEM((SLOTS,), jnp.int32),
                pltpu.SMEM((SLOTS,), jnp.int32),
                pltpu.VMEM((2 * SLOTS, LANES), F32),
                pltpu.VMEM((48, 2 * SLOTS), BF16),
                pltpu.VMEM((2, BLK, 8, LANES), F32),
                pltpu.VMEM((9 * BLK, 8, LANES), F32),
                pltpu.VMEM((2, 8, LANES), F32),
                pltpu.VMEM((18, 8, LANES), F32),
                pltpu.VMEM((BLK, LANES, 48), BF16),
                pltpu.VMEM((9 * BLK, 48, 2 * LANES), BF16),
                pltpu.VMEM((9 * BLK, 16, LANES), BF16),
                pltpu.VMEM((4, 2 * SLOTS, LANES), F32),
                pltpu.VMEM((2, 9, 4, BLK, LANES), F32),
                pltpu.VMEM((2, 9, 4, BLK, LANES), F32),
                pltpu.VMEM((2, 8 if n_dom % 8 == 0 else n_dom, 8, LANES), F32),
                pltpu.VMEM((2, 2 * (n_dom // 8 if n_dom % 8 == 0 else 1), 8, LANES), F32),
                pltpu.VMEM((2, n_slab, 8, LANES), F32),
                pltpu.VMEM((2, 48, segs), BF16),
                pltpu.VMEM((3, BLK, LANES), F32),
                pltpu.VMEM((5, BLK, 8, LANES), F32),
                pltpu.VMEM((3, BLK, LANES), F32),
                pltpu.VMEM((BLK, LANES), F32),
                pltpu.SemaphoreType.DMA((2, 6)),
                pltpu.SemaphoreType.DMA((2, 6)),
            ],
            compiler_params=pltpu.CompilerParams(collective_id=0, has_side_effects=True),
        )(positions, burgers, mobility.reshape(1, -1), block_cells, pairs.T, pair_count)
        return (positions + 0.5 * time_increment * total, 0.5 * total)

    placed = (
        P(None, ("slab", "dom")),
        P(None, ("slab", "dom")),
        P(("slab", "dom")),
        P(("slab", "dom")),
        P(("slab", "dom"), None),
        P(("slab", "dom")),
    )
    return jax.shard_map(
        body,
        mesh=mesh,
        in_specs=placed,
        out_specs=(P(None, ("slab", "dom")), P(None, ("slab", "dom"))),
        check_vma=False,
    )
```

```python
import functools
import math

import jax
import jax.numpy as jnp
from jax import lax
from jax.experimental import pallas as pl
from jax.experimental.pallas import tpu as pltpu
from jax.sharding import PartitionSpec as P

MESH = pl.DeviceIdType.MESH
F32 = jnp.float32
BF16 = jnp.bfloat16

BLK = 4
LANES = 128
SLOTS = 64
OWN = 16
UNROLL = 16
FIRST_PART = 48
NEAR_Z = 2
core_far = 9.0
time_increment = 0.25
around = [(-1, -1), (-1, 1), (1, -1), (1, 1), (0, -1), (0, 1), (-1, 0), (1, 0)]


def split3(x):
    hi = x.astype(BF16).astype(F32)
    rest = x - hi
    mid = rest.astype(BF16).astype(F32)
    return hi, mid, rest - mid


def left_stack(parts):
    hi, mid, lo = parts
    return jnp.concatenate([hi, hi, mid, hi, mid, lo], axis=0)


def right_stack(parts):
    hi, mid, lo = parts
    return jnp.concatenate([hi, mid, hi, lo, mid, hi], axis=0)


def mm(a, b, ca=1, cb=0):
    return lax.dot_general(a, b, (((ca,), (cb,)), ((), ())), preferred_element_type=F32)


def iotas():
    row = lax.broadcasted_iota(jnp.int32, (8, LANES), 0)
    lane = lax.broadcasted_iota(jnp.int32, (8, LANES), 1)
    return row, lane


def step_kernel(
    n_slab,
    n_dom,
    far_scale,
    pos_ref,
    bur_ref,
    mob_ref,
    cells_ref,
    pairs_ref,
    count_ref,
    out_ref,
    idx_a,
    idx_b,
    onehot,
    onehot_t,
    own,
    window,
    own_next,
    window_next,
    left_feat,
    right_feat,
    sums_feat,
    pair_sums,
    give,
    given,
    mom_y,
    mom_xc,
    mom_slab,
    bur_split,
    far_buf,
    far_geo,
    pos_rows,
    mob_rows,
    send_sem,
    recv_sem,
):
    s = lax.axis_index("slab")
    e = lax.axis_index("dom")
    row, lane = iotas()
    centre_x = (4 * s + 2).astype(F32)
    centre = jnp.where(row == 0, centre_x, jnp.where(row < 3, 4.0, 0.0))

    def peer(ds, de):
        return (lax.rem(s + ds + n_slab, n_slab), lax.rem(e + de + n_dom, n_dom))

    ny = 8 if n_dom % 8 == 0 else n_dom
    nx = n_dom // ny
    nz = n_slab // 2
    x, y, z, core = e // ny, e % ny, s // 2, s % 2
    far_first = lambda n: sorted(range(1, n), key=lambda i: -min(i, n - i))
    y_peers = [(s, x * ny + lax.rem(y + i, ny)) for i in far_first(ny)]
    xc_peers = [
        (2 * z + lax.rem(core + c, 2), lax.rem(x + i, nx) * ny + y)
        for i in far_first(nx) + [0]
        for c in range(2)
        if (i, c) != (0, 0)
    ]
    z_peers = [(2 * lax.rem(z + i, nz) + core, e) for i in far_first(nz)]

    barrier = pltpu.get_barrier_semaphore()

    def greet(slab, dom):
        pl.semaphore_signal(barrier, inc=1, device_id=(slab, dom), device_id_type=MESH)

    for group in (y_peers, xc_peers, z_peers):
        for slab, dom in group:
            greet(slab, dom)
    for ds, de in around:
        greet(*peer(ds, de))

    device = s * n_dom + e
    used = count_ref[0]

    def place(t, c):
        first = pairs_ref[0, t]
        second = pairs_ref[1, t]
        owner = second // BLK
        row_off = owner // n_dom - s + 1
        col_off = owner % n_dom - e + 1
        ia = jnp.clip(first - device * BLK, 0, BLK - 1)
        ib = jnp.clip((row_off * 3 + col_off) * BLK + second % BLK, 0, 9 * BLK - 1)
        idx_a[t] = ia
        idx_b[t] = ib
        live = t < used
        to_a = jnp.where(live, OWN + ia, LANES - 1)
        to_b = jnp.where(live, ib, LANES - 1)
        one_lane = lax.broadcasted_iota(jnp.int32, (1, LANES), 1)
        onehot[pl.ds(t, 1), :] = jnp.where(one_lane == to_a, 1.0, 0.0)
        onehot[pl.ds(SLOTS + t, 1), :] = jnp.where(one_lane == to_b, 1.0, 0.0)
        return c

    bur_tiles = []
    for b in range(BLK):
        cols = slice(b * LANES, (b + 1) * LANES)
        bur = bur_ref[:, cols]
        bur_tiles.append(bur)
        for c in range(3):
            pos_rows[c, b : b + 1, :] = pos_ref[c : c + 1, cols]
        mob_rows[b : b + 1, :] = mob_ref[:, cols]

    def set_up():
        lax.fori_loop(0, SLOTS, place, 0)
        onehot_t[...] = jnp.transpose(onehot[...])[:48].astype(BF16)
        blank = jnp.zeros((3, LANES), F32)
        for b, bur in enumerate(bur_tiles):
            cols = slice(b * LANES, (b + 1) * LANES)
            upper = jnp.concatenate([bur, blank, blank[0:2]], axis=0)
            lower = jnp.concatenate([blank, bur, blank[0:2]], axis=0)
            bur_split[0, :, cols] = right_stack(split3(upper)).astype(BF16)
            bur_split[1, :, cols] = right_stack(split3(lower)).astype(BF16)

    def local_moments(phase):
        sums = [jnp.zeros((8, LANES), F32) for _ in range(6)]
        for b in range(BLK):
            tile = own[phase, b]
            inside = cells_ref[b] - 16 * s
            zy = (2 * (inside // 4) + 1).astype(F32)
            zz = (2 * (inside % 4) + 1).astype(F32)
            d0 = tile[0:1] - centre_x
            d1 = tile[1:2] - zy
            d2 = tile[2:3] - zz
            one = jnp.ones((1, LANES), F32)
            squares = [3.0 * d * d for d in (d0, d1, d2)]
            mono = jnp.concatenate([one, d0, d1, d2, *squares, 3.0 * d0 * d1], axis=0)
            trace = -0.5 * (squares[0] + squares[1] + squares[2])
            more = jnp.concatenate(
                [3.0 * d0 * d2, 3.0 * d1 * d2, trace, jnp.zeros((5, LANES), F32)], axis=0
            )
            spot = lane == 16 * row + inside
            for k in range(3):
                bk = tile[3 + k : 4 + k]
                m = jnp.sum(mono * bk, axis=1, keepdims=True)
                sums[k] = sums[k] + jnp.where(spot, m, 0.0)
                m = jnp.sum(more * bk, axis=1, keepdims=True)
                sums[3 + k] = sums[3 + k] + jnp.where(spot, m, 0.0)
        rows = [jnp.sum(m, axis=0, keepdims=True) for m in sums]
        mom_y[phase, y] = jnp.concatenate(rows + [jnp.zeros((2, LANES), F32)], axis=0)

    def remote(src, dst, phase, kind, target):
        return pltpu.make_async_remote_copy(
            src_ref=src,
            dst_ref=dst,
            send_sem=send_sem.at[phase, kind],
            recv_sem=recv_sem.at[phase, kind],
            device_id=target,
            device_id_type=MESH,
        )

    def start_halo(phase):
        for ds, de in around:
            slot = (1 - ds) * 3 + (1 - de)
            if phase == 0:
                src, dst = own.at[0], window.at[pl.ds(slot * BLK, BLK)]
            else:
                src, dst = own_next, window_next.at[pl.ds(slot * 2, 2)]
            remote(src, dst, phase, 0, peer(ds, de)).start()

    def start_y(phase):
        mine = mom_y.at[phase, y]
        for target in y_peers:
            remote(mine, mine, phase, 1, target).start()

    def start_xc(phase):
        all_of(phase, 1).wait_recv()
        mom_xc[phase, 2 * x + core] = jnp.sum(mom_y[phase], axis=0)
        mine = mom_xc.at[phase, 2 * x + core]
        for target in xc_peers:
            remote(mine, mine, phase, 2, target).start()

    def start_z(phase):
        all_of(phase, 2).wait_recv()
        for c in range(2):
            parts = [mom_xc[phase, 2 * i + c] for i in range(nx)]
            mom_slab[phase, 2 * z + c] = sum(parts[1:], parts[0])
        mine = mom_slab.at[phase, pl.ds(2 * z, 2)]
        for i, target in zip(far_first(nz), z_peers):
            remote(mine, mine, phase, 3 if min(i, nz - i) <= NEAR_Z else 5, target).start()

    def start_give(phase):
        for ds, de in around:
            d = (ds + 1) * 3 + de + 1
            remote(give.at[phase, d], given.at[phase, 8 - d], phase, 4, peer(ds, de)).start()

    def extent(phase, kind):
        return (
            window.at[pl.ds(0, 8 * BLK)] if phase == 0 else window_next.at[pl.ds(0, 16)],
            mom_y.at[phase, pl.ds(0, ny - 1)],
            mom_xc.at[phase, pl.ds(0, 2 * nx - 1)],
            mom_slab.at[phase, pl.ds(0, 4 * NEAR_Z)],
            given.at[phase, pl.ds(0, 8)],
            mom_slab.at[phase, pl.ds(0, 2 * (nz - 1) - 4 * NEAR_Z)],
        )[kind]

    def all_of(phase, kind):
        whole = extent(phase, kind)
        return remote(whole, whole, phase, kind, peer(0, 1))

    def prepare(phase):
        def block(w, tile):
            r = tile - centre
            n = jnp.sum(jnp.where(row < 3, r * r, 0.0), axis=0, keepdims=True)
            mixed = jnp.where(row < 6, r, jnp.where(row == 6, n, 1.0))
            hi, mid, lo = split3(mixed)
            other = jnp.where(
                row < 3, -2.0 * r, jnp.where(row == 7, n + 0.25, jnp.where(row == 6, 1.0, 0.0))
            )
            right_feat[w, :, 0:LANES] = right_stack(split3(other)).astype(BF16)
            if phase == 0:
                is_b = (row >= 3) & (row < 6)
                bs = [jnp.where(is_b, part, 0.0) for part in (hi, mid, lo)]
                right_feat[w, :, LANES : 2 * LANES] = right_stack(bs).astype(BF16)
            sums_feat[w] = jnp.concatenate([hi, mid], axis=0).astype(BF16)

        def two(i, c):
            if phase == 0:
                first, second = window[2 * i], window[2 * i + 1]
            else:
                first = window_next[i]
                second = pltpu.roll(first, 4, 0)
            block(2 * i, first)
            block(2 * i + 1, second)
            return c

        lax.fori_loop(0, 9 * BLK // 2, two, 0, unroll=3)

    def prepare_own(phase, p):
        for c in range(3):
            far_buf[c] = p[c]
        for b in range(BLK):
            tile = own[phase, b]
            if phase == 0:
                window[OWN + b] = tile
        for half in range(2):
            if phase == 1:
                window_next[OWN // 2 + half] = own_next[half]
        zz = (2 * (row % 4) + 1).astype(F32)
        for t in range(BLK):
            dz = p[2][t : t + 1] - zz
            far_geo[2, t] = dz
            for par in range(2):
                dy = p[1][t : t + 1] - (2 * (2 * par + row // 4) + 1).astype(F32)
                far_geo[par, t] = dy
                far_geo[3 + par, t] = dy * dy + dz * dz + core_far
        for b in range(BLK):
            r = own[phase, b] - centre
            n = jnp.sum(jnp.where(row < 3, r * r, 0.0), axis=0, keepdims=True)
            mixed = jnp.where(row < 6, r, jnp.where(row == 6, n, 1.0))
            left_feat[b] = jnp.transpose(left_stack(split3(mixed))).astype(BF16)

    def near(begin, end):
        def pair(t):
            ia = idx_a[t]
            ib = idx_b[t]
            both = mm(left_feat[ia], right_feat[ib])
            close = both[:, 0:LANES]
            coef = both[:, LANES : 2 * LANES]
            r1 = lax.rsqrt(close)
            r2 = lax.rsqrt(close + (core_far - 0.25))
            w = coef * (r1 * r1 * r1 - r2 * r2 * r2)
            hi = w.astype(BF16)
            lo = (w - hi.astype(F32)).astype(BF16)
            fa = sums_feat[OWN + ia]
            fb = sums_feat[ib]
            for_b = jnp.concatenate([hi, lo], axis=0)
            for_a = jnp.concatenate([jnp.transpose(hi), jnp.transpose(lo)], axis=0)
            on_b = mm(jnp.concatenate([fa, fa], axis=1), for_b)
            on_a = mm(jnp.concatenate([fb, fb], axis=1), for_a)
            on_a = on_a[0:8] + on_a[8:16]
            on_b = on_b[0:8] + on_b[8:16]
            for i, r in enumerate((0, 1, 2, 7)):
                pair_sums[i, pl.ds(t, 1), :] = on_a[r : r + 1]
                pair_sums[i, pl.ds(SLOTS + t, 1), :] = on_b[r : r + 1]

        def turn(i, c):
            for u in range(UNROLL):
                pair(i * UNROLL + u)
            return c

        lax.fori_loop(begin // UNROLL, end // UNROLL, turn, 0)

    def collect(phase):
        chosen = onehot_t[...]
        acc = []
        for i in range(4):
            hi, mid, lo = split3(pair_sums[i])
            acc.append(mm(chosen, hi.astype(BF16)) + mm(chosen, mid.astype(BF16)) + mm(chosen, lo.astype(BF16)))
        blocks = lax.broadcasted_iota(jnp.int32, (48, LANES), 0)
        shift = (4 * (1 - blocks // 12)).astype(F32)
        acc[0] = acc[0] + shift * acc[3]
        for d in range(9):
            for i in range(4):
                give[phase, d, i] = acc[i][d * BLK : (d + 1) * BLK]

    def far(phase, begin, end, acc):
        def products(j):
            stacked = jnp.transpose(left_stack(split3(mom_slab[phase, j]))).astype(BF16)
            return mm(stacked, bur_split[0]), mm(stacked[0:48], bur_split[1])

        def forces(j, found, acc):
            q1, q2 = found
            zx = (4 * j + 2).astype(F32)
            for t in range(BLK):
                cols = slice(t * LANES, (t + 1) * LANES)
                dx = jnp.broadcast_to(far_buf[0, t : t + 1, :] - zx, (8, LANES))
                dx2 = dx * dx
                dz = far_geo[2, t]
                for par in range(2):
                    q = [q1[16 * f + 8 * par : 16 * f + 8 * par + 8, cols] for f in range(8)]
                    q += [q2[16 * f + 8 * par : 16 * f + 8 * par + 8, cols] for f in range(3)]
                    dy = far_geo[par, t]
                    rs = lax.rsqrt(dx2 + far_geo[3 + par, t])
                    i2 = rs * rs
                    i3 = rs * i2
                    tx = q[4] * dx + q[7] * dy + q[8] * dz
                    ty = q[7] * dx + q[5] * dy + q[9] * dz
                    tz = q[8] * dx + q[9] * dy + q[6] * dz
                    qr = q[1] * dx + q[2] * dy + q[3] * dz
                    rqr = tx * dx + ty * dy + tz * dz
                    scal = q[0] + i2 * (3.0 * qr + q[10] + 2.5 * i2 * rqr)
                    acc[t] = acc[t] + i3 * (dx * scal - q[1] - i2 * tx)
                    acc[4 + t] = acc[4 + t] + i3 * (dy * scal - q[2] - i2 * ty)
                    acc[8 + t] = acc[8 + t] + i3 * (dz * scal - q[3] - i2 * tz)
            return acc

        acc = list(acc)
        for i in range(begin, end):
            j = lax.rem(2 * (z + nz - NEAR_Z) + i, n_slab)
            acc = forces(j, products(j), acc)
        return acc

    def speed(phase):
        p = [far_buf[c] for c in range(3)]
        start_xc(phase)
        all_of(phase, 0).wait_recv()
        prepare(phase)
        near(0, FIRST_PART)
        start_z(phase)
        near(FIRST_PART, SLOTS)
        collect(phase)
        start_give(phase)
        zero = jnp.zeros((8, LANES), F32)
        middle = 4 * NEAR_Z + 2
        all_of(phase, 3).wait_recv()
        total = far(phase, 0, middle, [zero] * 12)
        all_of(phase, 5).wait_recv()
        total = far(phase, middle, n_slab, total)
        all_of(phase, 4).wait_recv()
        got = [give[phase, 4, i] for i in range(4)]
        for d in range(9):
            if d != 4:
                got = [got[i] + given[phase, d, i] for i in range(4)]
        v = []
        for c in range(3):
            fars = [jnp.sum(total[4 * c + t], axis=0, keepdims=True) for t in range(BLK)]
            near_c = (p[c] - (centre_x if c == 0 else 4.0)) * got[3] - got[c]
            v.append(mob_rows[...] * (far_scale * jnp.concatenate(fars, axis=0) + near_c))
        return v

    def publish(phase, p):
        for b in range(BLK):
            own[phase, b] = jnp.concatenate(
                [q[b : b + 1] for q in p] + [bur_tiles[b], jnp.zeros((2, LANES), F32)], axis=0
            )
        if phase == 1:
            blank = jnp.zeros((1, LANES), F32)
            for half in range(2):
                rows = []
                for b in (2 * half, 2 * half + 1):
                    rows += [q[b : b + 1] for q in p] + [blank]
                own_next[half] = jnp.concatenate(rows, axis=0)
        local_moments(phase)

    first_p = [pos_rows[c] for c in range(3)]
    publish(0, first_p)
    pl.semaphore_wait(barrier, len(y_peers) + len(xc_peers) + len(z_peers) + len(around))
    start_y(0)
    start_halo(0)
    set_up()
    prepare_own(0, first_p)
    first_v = speed(0)
    second_p = [p + time_increment * v for p, v in zip(first_p, first_v)]
    publish(1, second_p)
    start_y(1)
    start_halo(1)
    prepare_own(1, second_p)
    second_v = speed(1)
    for c in range(3):
        both = first_v[c] + second_v[c]
        for b in range(BLK):
            out_ref[c : c + 1, b * LANES : (b + 1) * LANES] = both[b : b + 1]
    for phase in range(2):
        for kind in range(6):
            all_of(phase, kind).wait_send()


def solution(mesh):
    n_slab = mesh.shape["slab"]
    n_dom = mesh.shape["dom"]

    def body(positions, burgers, mobility, block_cells, pairs, pair_count):
        segs = positions.shape[1]
        far_scale = math.sqrt(16 * n_slab / (segs * n_slab * n_dom))
        vmem = pl.BlockSpec(memory_space=pltpu.VMEM)
        smem = pl.BlockSpec(memory_space=pltpu.SMEM)
        total = pl.pallas_call(
            functools.partial(step_kernel, n_slab, n_dom, far_scale),
            out_shape=jax.ShapeDtypeStruct((3, segs), F32),
            in_specs=[vmem, vmem, vmem, smem, smem, smem],
            out_specs=vmem,
            scratch_shapes=[
                pltpu.SMEM((SLOTS,), jnp.int32),
                pltpu.SMEM((SLOTS,), jnp.int32),
                pltpu.VMEM((2 * SLOTS, LANES), F32),
                pltpu.VMEM((48, 2 * SLOTS), BF16),
                pltpu.VMEM((2, BLK, 8, LANES), F32),
                pltpu.VMEM((9 * BLK, 8, LANES), F32),
                pltpu.VMEM((2, 8, LANES), F32),
                pltpu.VMEM((18, 8, LANES), F32),
                pltpu.VMEM((BLK, LANES, 48), BF16),
                pltpu.VMEM((9 * BLK, 48, 2 * LANES), BF16),
                pltpu.VMEM((9 * BLK, 16, LANES), BF16),
                pltpu.VMEM((4, 2 * SLOTS, LANES), F32),
                pltpu.VMEM((2, 9, 4, BLK, LANES), F32),
                pltpu.VMEM((2, 9, 4, BLK, LANES), F32),
                pltpu.VMEM((2, 8 if n_dom % 8 == 0 else n_dom, 8, LANES), F32),
                pltpu.VMEM((2, 2 * (n_dom // 8 if n_dom % 8 == 0 else 1), 8, LANES), F32),
                pltpu.VMEM((2, n_slab, 8, LANES), F32),
                pltpu.VMEM((2, 48, segs), BF16),
                pltpu.VMEM((3, BLK, LANES), F32),
                pltpu.VMEM((5, BLK, 8, LANES), F32),
                pltpu.VMEM((3, BLK, LANES), F32),
                pltpu.VMEM((BLK, LANES), F32),
                pltpu.SemaphoreType.DMA((2, 6)),
                pltpu.SemaphoreType.DMA((2, 6)),
            ],
            compiler_params=pltpu.CompilerParams(collective_id=0, has_side_effects=True),
        )(positions, burgers, mobility.reshape(1, -1), block_cells, pairs.T, pair_count)
        return (positions + 0.5 * time_increment * total, 0.5 * total)

    placed = (
        P(None, ("slab", "dom")),
        P(None, ("slab", "dom")),
        P(("slab", "dom")),
        P(("slab", "dom")),
        P(("slab", "dom"), None),
        P(("slab", "dom")),
    )
    return jax.shard_map(
        body,
        mesh=mesh,
        in_specs=placed,
        out_specs=(P(None, ("slab", "dom")), P(None, ("slab", "dom"))),
        check_vma=False,
    )
```
